512 devices in a mesh: leaf: 32 (over z, core), front: 16 (over y, x).
Axes of the slice: x: 4, y: 4, z: 16, core: 2. Of those that a mesh axis runs over, the one named last changes fastest.
Arguments:
- parent_border_inverse: float32 [32, 1536, 1536], P('leaf', 'front')
- parent_border_rows: float32 [32, 1536, 768], P('leaf', 'front'), may hold values from -0.09 to 0.09
- parent_diagonal_inverse: float32 [32, 768, 768], P('leaf', 'front')
- child_border_rows: float32 [64, 1024, 512], P('leaf', 'front'), may hold values from -0.13 to 0.13
- child_factor_inverse: float32 [64, 512, 512], P('leaf', 'front')
- child_index: int32 [64, 1024], replicated, may hold values from 0 to 2303, as said below
- child_parent: int32 [64], replicated, may hold values from 0 to 31, as said below
Outputs:
- parent_variance: float32 [32, 768], P('leaf')
- child_variance: float32 [64, 512], P('leaf')
The draws below stay inside these ranges and needn't reach their ends.
Inputs may be any that keep to these rules, and one draw needn't show every extreme that they name: `child_index`: each row holds 1024 distinct positions in increasing order, the first 0 and the last 2303. `child_parent`: child c's parent is c // 2 or c // 2 with its lowest bit flipped, and every parent has exactly two children.
All inputs are finite; a program needn't handle non-finite values.
Results may differ from the reference program's by a relative error of at most 0.0003.
Values sent between devices are 32-bit elements; how exact they have to be, the bound alone decides.
A program may use at most 64 MiB of HBM per device.

```python
import math
import jax
import jax.numpy as jnp
from jax import lax

ELIMINATED_SIZE = 768
BORDER_SIZE = 1536
CHILD_ELIMINATED = 512
CHILD_BORDER = 1024
PARENT_FRONTS = 32
CHILD_FRONTS = 64


def inverse_lower(key, count, size, spread):
    first, second = jax.random.split(key)
    noise = jax.random.normal(first, (count, size, size), jnp.float32) * spread
    rowpos = jnp.arange(size)[:, None]
    colpos = jnp.arange(size)[None, :]
    strict = (rowpos > colpos).astype(jnp.float32)
    eye_mask = (rowpos == colpos).astype(jnp.float32)
    diagonal = jnp.exp(jax.random.uniform(second, (count, size), jnp.float32, math.log(0.5), math.log(1.5)))
    return noise * strict[None] + eye_mask[None] * diagonal[:, :, None]


def draw_parent_border_inverse(key, part):
    first, second = jax.random.split(key, 2)
    noise = jax.random.normal(first, (PARENT_FRONTS, BORDER_SIZE, BORDER_SIZE), jnp.float32)
    symmetric = (noise + jnp.transpose(noise, (0, 2, 1))) * (0.6 / math.sqrt(BORDER_SIZE))
    diagonal = jnp.exp(jax.random.uniform(second, (PARENT_FRONTS, BORDER_SIZE), jnp.float32, math.log(2.5), math.log(7.0)))
    eye_mask = (jnp.arange(BORDER_SIZE)[:, None] == jnp.arange(BORDER_SIZE)[None, :]).astype(jnp.float32)
    result = symmetric + eye_mask[None] * diagonal[:, :, None]
    return result


def draw_parent_diagonal_inverse(key, part):
    return inverse_lower(key, PARENT_FRONTS, ELIMINATED_SIZE, 0.02)


def draw_child_factor_inverse(key, part):
    return inverse_lower(key, CHILD_FRONTS, CHILD_ELIMINATED, 0.025)


def draw_child_index(key, part):
    random_keys = jax.random.split(jax.random.fold_in(key, 11), CHILD_FRONTS)
    front_orders = jax.vmap(lambda single_front: jax.random.permutation(single_front, ELIMINATED_SIZE + BORDER_SIZE - 2))(random_keys)
    middle = front_orders[:, :CHILD_BORDER - 2].astype(jnp.int32) + 1
    first_col = jnp.zeros((CHILD_FRONTS, 1), jnp.int32)
    final_column = jnp.full((CHILD_FRONTS, 1), ELIMINATED_SIZE + BORDER_SIZE - 1, jnp.int32)
    return jnp.sort(jnp.concatenate([first_col, middle, final_column], axis=1), axis=1).astype(jnp.int32)


def draw_child_parent(key, part):
    groups = CHILD_FRONTS // 4
    random_keys = jax.random.split(jax.random.fold_in(key, 23), groups)
    perms = jax.vmap(lambda single_front: jax.random.permutation(single_front, 4))(random_keys).astype(jnp.int32)
    group = jnp.arange(groups, dtype=jnp.int32)[:, None]
    targets = (4 * group + perms).reshape(-1)
    values = (2 * group + jnp.array([0, 0, 1, 1], jnp.int32)[None, :]).reshape(-1)
    return jnp.zeros((CHILD_FRONTS,), jnp.int32).at[targets].set(values).astype(jnp.int32)


def block_levels(stream_key, shape, cuts, least, top_value):
    def one(axis_at, shards_of):
        steps = jax.random.uniform(jax.random.fold_in(jax.random.fold_in(stream_key, 6), axis_at), (shards_of,), jnp.float32, least / len(cuts), top_value / len(cuts))
        return jnp.repeat(jnp.exp(steps), shape[axis_at] // shards_of).reshape((-1,) + (1,) * (len(shape) - axis_at - 1))

    loudness = one(*cuts[0])
    for cut in cuts[1:]:
        loudness = loudness * one(*cut)
    return loudness


def normal_values(stream_key, extent, scale, most, cuts=(), kind=jnp.bfloat16):
    values = jax.random.normal(stream_key, extent, jnp.float32) * scale
    if len(cuts) > 0:
        values = block_levels(stream_key, extent, cuts, -0.22, 0.18) * values
    return jnp.clip(values, min=-most, max=most).astype(kind)


def setup_inputs(seed: int = 0) -> dict:
    keys = jax.random.split(jax.random.key(seed), 8)
    parent_border_inverse = draw_parent_border_inverse(jax.random.fold_in(keys[7], 71), 0)
    parent_border_rows = normal_values(keys[1], (PARENT_FRONTS, BORDER_SIZE, ELIMINATED_SIZE), 0.015, 0.09, ((0, 32), (1, 16)), jnp.float32)
    parent_diagonal_inverse = draw_parent_diagonal_inverse(jax.random.fold_in(keys[7], 71), 0)
    child_border_rows = normal_values(keys[3], (CHILD_FRONTS, CHILD_BORDER, CHILD_ELIMINATED), 0.022, 0.13, ((0, 32), (1, 16)), jnp.float32)
    child_factor_inverse = draw_child_factor_inverse(jax.random.fold_in(keys[7], 71), 0)
    child_index = draw_child_index(jax.random.fold_in(keys[7], 71), 0)
    child_parent = draw_child_parent(jax.random.fold_in(keys[7], 71), 0)
    return {"parent_border_inverse": parent_border_inverse, "parent_border_rows": parent_border_rows, "parent_diagonal_inverse": parent_diagonal_inverse, "child_border_rows": child_border_rows, "child_factor_inverse": child_factor_inverse, "child_index": child_index, "child_parent": child_parent}


def matrix_product(left, right):
    return jnp.dot(left, right, precision=lax.Precision.HIGHEST, preferred_element_type=jnp.float32)


def children_of(child_parent, owner):
    partner = jnp.bitwise_xor(owner, 1)
    pool_ids = jnp.stack([2 * owner, 2 * owner + 1, 2 * partner, 2 * partner + 1]).astype(jnp.int32)
    member = (jnp.take(child_parent, pool_ids) == owner).astype(jnp.int32)
    first = jnp.argmax(member).astype(jnp.int32)
    second = (3 - jnp.argmax(member[::-1])).astype(jnp.int32)
    slots = jnp.stack([first, second]).astype(jnp.int32)
    return slots, jnp.take(pool_ids, slots).astype(jnp.int32)


def paired_fronts(border_inverse, border_factor, eliminated_inverse, child_factors, child_inverses, index_list):
    weight_rows = matrix_product(border_factor, eliminated_inverse)
    border_product = matrix_product(border_inverse, weight_rows)
    parent_marginal = jnp.sum(eliminated_inverse * eliminated_inverse, axis=0) + jnp.sum(weight_rows * border_product, axis=0)
    quadratic_terms = []
    for child_front in range(2):
        child_weight = matrix_product(child_factors[child_front], child_inverses[child_front])
        placed_rows = jnp.zeros((ELIMINATED_SIZE + BORDER_SIZE, CHILD_ELIMINATED), jnp.float32).at[index_list[child_front]].set(child_weight)
        upper_block = placed_rows[:ELIMINATED_SIZE]
        lower_block = placed_rows[ELIMINATED_SIZE:]
        reduced = lower_block - matrix_product(weight_rows, upper_block)
        kid_image = matrix_product(border_inverse, reduced)
        lifted_rows = matrix_product(eliminated_inverse, upper_block)
        quadratic_terms.append(jnp.sum(lifted_rows * lifted_rows, axis=0) + jnp.sum(reduced * kid_image, axis=0))
    return parent_marginal, jnp.stack(quadratic_terms)


def reference(parent_border_inverse, parent_border_rows, parent_diagonal_inverse, child_border_rows, child_factor_inverse, child_index, child_parent):
    counter = jnp.arange(PARENT_FRONTS, dtype=jnp.int32)

    def one_parent(position):
        slots, child_fronts = children_of(child_parent, position)
        parent_marginal, quadratic_terms = paired_fronts(parent_border_inverse[position], parent_border_rows[position],
                                       parent_diagonal_inverse[position], child_border_rows[child_fronts],
                                       child_factor_inverse[child_fronts], child_index[child_fronts])
        return parent_marginal, quadratic_terms, child_fronts

    parent_marginal, quadratic_terms, child_fronts = lax.map(one_parent, counter)
    own_term = jnp.sum(child_factor_inverse * child_factor_inverse, axis=1)
    placed_quadratics = jnp.zeros((CHILD_FRONTS, CHILD_ELIMINATED), jnp.float32).at[child_fronts.reshape(-1)].set(quadratic_terms.reshape(-1, CHILD_ELIMINATED))
    return parent_marginal, own_term + placed_quadratics
```

```python
import jax
import jax.numpy as jnp
from jax import lax
from jax.experimental import pallas as pl
from jax.experimental.pallas import tpu as pltpu
from jax.sharding import PartitionSpec as P

F32 = jnp.float32
BF16 = jnp.bfloat16
MESH = pl.DeviceIdType.MESH


def dot(a, b):
    return jnp.dot(a, b, preferred_element_type=F32)


def dot3(ah, al, bh, bl):
    return dot(ah, bh) + (dot(ah, bl) + dot(al, bh))


def split(x):
    hi = x.astype(BF16)
    return hi, (x - hi.astype(F32)).astype(BF16)


def col_sum(x):
    return jnp.sum(x, axis=0, keepdims=True)


def select(flag, yes, no):
    return jnp.where(jnp.full(yes.shape, flag, jnp.int32) == 1, yes, no)


def kernel(
    b_in, f_in, d_in, cf_in, e_in, idx_in, owner,
    out_p, out_c,
    b_s, f_s, d_s, cf_s, e_s, k_own, k_par, k_s, v_s, r_s, idx_s, l_s,
    su, sl, bh, bl, fh, fl, dh, dl, ch, cl, eh, el, kh, kl, uh, ul, vh, vl, rh, rl,
    stage, fin, ostage, xfin, send, recv, loc,
):
    leaf = lax.axis_index("leaf")
    front = lax.axis_index("front")
    y = lax.div(front, 4)
    x = lax.rem(front, 4)
    partner = leaf + 1 - 2 * lax.rem(leaf, 2)
    count = [0]
    copies = []

    def remote(src, dst, device):
        k = count[0]
        count[0] += 1
        copy = pltpu.make_async_remote_copy(
            src_ref=src, dst_ref=dst, send_sem=send.at[k], recv_sem=recv.at[k],
            device_id=device, device_id_type=MESH,
        )
        copies.append(copy)
        return copy

    def at_x(p):
        return {"front": y * 4 + p}

    def at_y(p):
        return {"front": p * 4 + x}

    class Ring:
        def __init__(self, device, pos, slot, half, own=None):
            right, left = lax.rem(pos + 1, 4), lax.rem(pos + 3, 4)
            own = slot(pos) if own is None else own
            self.first_r = remote(own, slot(pos), device(right))
            self.first_l = remote(own, slot(pos), device(left))
            self.next_r = remote(half(left, 0), half(left, 0), device(right))
            self.next_l = remote(half(right, 1), half(right, 1), device(left))

        def begin(self):
            self.first_r.start()
            self.first_l.start()

        def relay(self):
            self.first_r.wait_recv()
            self.next_r.start()
            self.first_l.wait_recv()
            self.next_l.start()

        def finish(self):
            self.next_r.wait_recv()
            self.next_l.wait_recv()

    def rows(ref, size):
        return lambda p: ref.at[pl.ds(p * size, size), :]

    def half_rows(ref, size):
        return lambda p, h: ref.at[pl.ds(p * size + h * (size // 2), size // 2), :]

    def stacked(ref, base, size):
        return lambda p: ref.at[pl.ds(base, 2), pl.ds(p * size, size), :]

    def half_stacked(ref, base, size):
        return lambda p, h: ref.at[base + h, pl.ds(p * size, size), :]

    def tile(ref, t, size):
        return lambda p: ref.at[t, pl.ds(p * size, size), :]

    def half_tile(ref, t, size):
        return lambda p, h: ref.at[t, pl.ds(p * size + h * (size // 2), size // 2), :]

    barrier = pltpu.get_barrier_semaphore()
    peers = [at_x(lax.rem(x + d, 4)) for d in (1, 2, 3)]
    peers += [at_y(lax.rem(y + d, 4)) for d in (1, 2, 3)]
    peers += [
        {"leaf": partner, "front": lax.rem(y + d, 4) * 4 + x} for d in (0, 1, 2, 3)
    ]
    for peer in peers:
        pl.semaphore_signal(barrier, inc=1, device_id=peer, device_id_type=MESH)

    locals_ = [
        (e_in.at[:, :, pl.ds(pl.multiple_of(x * 128, 128), 128)], e_s.at[:, pl.ds(y * 128 + x * 32, 32), :]),
        (d_in, d_s.at[pl.ds(x * 48, 48), :]),
        (cf_in, cf_s.at[:, pl.ds(x * 64, 64), :]),
        (f_in, f_s.at[pl.ds(x * 96, 96), :]),
        (b_in, b_s.at[pl.ds(x * 96, 96), :]),
        (idx_in.at[pl.ds(pl.multiple_of(lax.div(leaf, 4) * 8, 8), 8), :], idx_s),
    ]
    own_e, own_d, own_cf, own_f, own_b, own_idx = [
        pltpu.make_async_copy(src, dst, loc.at[i]) for i, (src, dst) in enumerate(locals_)
    ]
    for copy in (own_e, own_d, own_cf, own_f, own_b, own_idx):
        copy.start()

    e_across = []
    for d in (1, 2, 3):
        other = lax.rem(x + d, 4)
        e_across.append(remote(
            e_in.at[:, :, pl.ds(pl.multiple_of(other * 128, 128), 128)],
            e_s.at[:, pl.ds(y * 128 + x * 32, 32), :],
            at_x(other),
        ))
    ring_d = Ring(at_x, x, rows(d_s, 48), half_rows(d_s, 48), d_in)
    ring_cf = Ring(at_x, x, stacked(cf_s, 0, 64), half_stacked(cf_s, 0, 64), cf_in)
    ring_f = Ring(at_x, x, rows(f_s, 96), half_rows(f_s, 96), f_in)
    ring_b = Ring(at_x, x, rows(b_s, 96), half_rows(b_s, 96), b_in)
    ring_e = Ring(at_y, y, stacked(e_s, 0, 128), half_stacked(e_s, 0, 128))
    ring_dp = Ring(at_y, y, stacked(v_s, 0, 192), half_stacked(v_s, 0, 192))
    ring_k = Ring(at_y, y, stacked(k_s, 0, 256), half_stacked(k_s, 0, 256))
    ring_v = Ring(at_y, y, stacked(v_s, 2, 192), half_stacked(v_s, 2, 192))
    ring_w0 = Ring(at_y, y, tile(r_s, 0, 384), half_tile(r_s, 0, 384))
    ring_w1 = Ring(at_y, y, tile(r_s, 1, 384), half_tile(r_s, 1, 384))
    ring_r = Ring(at_y, y, stacked(r_s, 2, 384), half_stacked(r_s, 2, 384))
    k_cross = remote(k_own, k_par, {"leaf": partner})

    pl.semaphore_wait(barrier, 10)

    for copy in e_across:
        copy.start()
    ring_d.begin()
    ring_cf.begin()

    pool = (2 * leaf, 2 * leaf + 1, 2 * partner, 2 * partner + 1)
    mine = [(owner[p] == leaf).astype(jnp.int32) for p in pool]
    theirs = [1 - m for m in mine]
    own_idx.wait()
    in_eight = [lax.rem(p, 8) for p in pool]
    idx_rows = [idx_s[pl.ds(p, 1), :] for p in in_eight]
    first_idx = select(mine[0], idx_rows[0], select(mine[1], idx_rows[1], idx_rows[2]))
    last_idx = select(mine[3], idx_rows[3], select(mine[2], idx_rows[2], idx_rows[1]))

    def one_hot(c, positions):
        for m in range(0, 768, 128):
            at = lax.broadcasted_iota(jnp.int32, (128, 1024), 0) + m
            su[c, pl.ds(m, 128), :] = jnp.where(at == positions, 1.0, 0.0).astype(BF16)
        for m in range(0, 384, 128):
            at = lax.broadcasted_iota(jnp.int32, (128, 1024), 0) + (768 + 384 * y + m)
            sl[c, pl.ds(m, 128), :] = jnp.where(at == positions, 1.0, 0.0).astype(BF16)

    def split_rows(src, hi, lo, size, step):
        for m in range(0, size, step):
            h, l = split(src[pl.ds(m, step), :])
            hi[pl.ds(m, step), :] = h
            lo[pl.ds(m, step), :] = l

    own_e.wait()
    for copy in e_across:
        copy.wait_recv()
    ring_e.begin()
    one_hot(0, first_idx)
    ring_d.relay()
    ring_e.relay()
    one_hot(1, last_idx)
    ring_cf.relay()
    ring_f.begin()

    own_d.wait()
    ring_d.finish()
    window = (x + lax.div(x, 2)) * 128
    d_sums = []
    for t in range(2):
        part = d_s[:, pl.ds(pl.multiple_of(window + t * 128, 128), 128)]
        v_s[t, pl.ds(pl.multiple_of(y * 192, 192), 192), :] = part
        d_sums.append(col_sum(part * part))
    ring_dp.begin()
    split_rows(d_s, dh, dl, 192, 48)

    ring_e.finish()
    e_sums = []
    for c in range(2):
        for m in range(0, 512, 128):
            h, l = split(e_s[c, pl.ds(m, 128), :])
            eh[c, pl.ds(m, 128), :] = h
            el[c, pl.ds(m, 128), :] = l
        part = e_s[c, pl.ds(pl.multiple_of(y * 128, 128), 128), :]
        e_sums.append(col_sum(part * part))
    own_cf.wait()
    ring_cf.finish()
    for c in range(2):
        for m in range(0, 256, 64):
            h, l = split(cf_s[c, pl.ds(m, 64), :])
            ch[c, pl.ds(m, 64), :] = h
            cl[c, pl.ds(m, 64), :] = l
        for m in range(0, 256, 128):
            at = pl.ds(m, 128)
            k_own[c, at, :] = dot3(ch[c, at, :], cl[c, at, :], eh[c], el[c])
    k_cross.start()
    ring_dp.relay()
    k_cross.wait_recv()
    for m in range(0, 256, 64):
        at = pl.ds(m, 64)
        pooled = [k_own[0, at, :], k_own[1, at, :], k_par[0, at, :], k_par[1, at, :]]
        to = pl.ds(pl.multiple_of(y * 256 + m, 64), 64)
        k_s[0, to, :] = select(mine[0], pooled[0], select(mine[1], pooled[1], pooled[2]))
        k_s[1, to, :] = select(mine[3], pooled[3], select(mine[2], pooled[2], pooled[1]))
    ring_k.begin()
    ring_f.relay()
    ring_b.begin()

    def split_v(base):
        for t in range(2):
            for m in range(0, 768, 128):
                h, l = split(v_s[base + t, pl.ds(m, 128), :])
                vh[pl.ds(m, 128), pl.ds(t * 128, 128)] = h
                vl[pl.ds(m, 128), pl.ds(t * 128, 128)] = l

    ring_dp.finish()
    split_v(0)
    ring_k.relay()
    own_f.wait()
    ring_f.finish()
    split_rows(f_s, fh, fl, 384, 48)
    for m in range(0, 384, 128):
        at = pl.ds(m, 128)
        value = dot3(fh[at, :], fl[at, :], vh[...], vl[...])
        to = pl.ds(pl.multiple_of(y * 384 + m, 128), 128)
        r_s[0, to, :] = value[:, :128]
        r_s[1, to, :] = value[:, 128:]
    ring_w0.begin()

    ring_k.finish()
    for c in range(2):
        for m in range(0, 1024, 128):
            h, l = split(k_s[c, pl.ds(m, 128), :])
            kh[c, pl.ds(m, 128), :] = h
            kl[c, pl.ds(m, 128), :] = l
        for m in range(0, 768, 256):
            at = pl.ds(m, 256)
            uh[at, pl.ds(c * 128, 128)] = dot(su[c, at, :], kh[c]).astype(BF16)
            ul[at, pl.ds(c * 128, 128)] = dot(su[c, at, :], kl[c]).astype(BF16)
    v_sums = [jnp.zeros((1, 128), F32)] * 2
    for m in range(0, 192, 96):
        at = pl.ds(m, 96)
        value = dot3(dh[at, :], dl[at, :], uh[...], ul[...])
        to = pl.ds(pl.multiple_of(y * 192 + m, 96), 96)
        for c in range(2):
            part = value[:, c * 128:(c + 1) * 128]
            v_s[2 + c, to, :] = part
            v_sums[c] = v_sums[c] + col_sum(part * part)
    ring_v.begin()
    ring_w0.relay()
    ring_v.relay()
    ring_w1.begin()
    for c in range(2):
        for m in range(0, 384, 128):
            at = pl.ds(m, 128)
            l_s[at, pl.ds(c * 128, 128)] = dot(sl[c, at, :], kh[c]) + dot(sl[c, at, :], kl[c])
    ring_b.relay()
    ring_v.finish()
    split_v(2)
    for m in range(0, 384, 128):
        at = pl.ds(m, 128)
        value = l_s[at, :] - dot3(fh[at, :], fl[at, :], vh[...], vl[...])
        to = pl.ds(pl.multiple_of(y * 384 + m, 128), 128)
        r_s[2, to, :] = value[:, :128]
        r_s[3, to, :] = value[:, 128:]
    ring_r.begin()
    ring_w1.relay()
    own_b.wait()
    ring_b.finish()
    split_rows(b_s, bh, bl, 384, 24)
    ring_r.relay()

    def quadratic(base):
        for t in range(2):
            for m in range(0, 1536, 128):
                h, l = split(r_s[base + t, pl.ds(m, 128), :])
                rh[pl.ds(m, 128), pl.ds(t * 128, 128)] = h
                rl[pl.ds(m, 128), pl.ds(t * 128, 128)] = l
        sums = [jnp.zeros((1, 128), F32)] * 2
        for m in range(0, 384, 128):
            at = pl.ds(m, 128)
            value = dot3(bh[at, :], bl[at, :], rh[...], rl[...])
            to = pl.ds(pl.multiple_of(y * 384 + m, 128), 128)
            for t in range(2):
                sums[t] = sums[t] + col_sum(value[:, t * 128:(t + 1) * 128] * r_s[base + t, to, :])
        return sums

    ring_w0.finish()
    ring_w1.finish()
    p_sums = quadratic(0)
    ring_r.finish()
    c_sums = quadratic(2)

    for t in range(2):
        stage[pl.ds(t, 1), :] = p_sums[t] + d_sums[t]
        stage[pl.ds(2 + t, 1), :] = c_sums[t] + v_sums[t]
        stage[pl.ds(4 + t, 1), :] = e_sums[t]
    stage[pl.ds(6, 2), :] = jnp.zeros((2, 128), F32)
    fin[0, y] = stage[...]
    ends = []
    for d in (1, 2, 3):
        ends.append(remote(stage, fin.at[0, y], at_y(lax.rem(y + d, 4))))
    for d in (0, 1, 2, 3):
        ends.append(remote(stage, fin.at[1, y], {"leaf": partner, "front": lax.rem(y + d, 4) * 4 + x}))
    for copy in ends:
        copy.start()
    for copy in ends:
        copy.wait_recv()
    own = ((fin[0, 0] + fin[0, 1]) + fin[0, 2]) + fin[0, 3]
    other = ((fin[1, 0] + fin[1, 1]) + fin[1, 2]) + fin[1, 3]
    before = theirs[2] * 0 + (1 - mine[2]) + (1 - mine[3])
    quad_0 = select(mine[0], own[2:3], select(before, other[3:4], other[2:3]))
    quad_1 = select(mine[1], select(mine[0], own[3:4], own[2:3]), other[3:4])
    ostage[0:2, :] = own[0:2]
    ostage[2:3, :] = own[4:5] + quad_0
    ostage[3:4, :] = own[5:6] + quad_1
    ostage[4:8, :] = jnp.zeros((4, 128), F32)
    xfin[x] = ostage[...]
    ends = []
    for d in (1, 2, 3):
        ends.append(remote(ostage, xfin.at[x], at_x(lax.rem(x + d, 4))))
    for copy in ends:
        copy.start()
    for copy in ends:
        copy.wait_recv()
    for t, (p, r) in enumerate(((0, 0), (0, 1), (1, 1), (2, 0), (2, 1), (3, 1))):
        out_p[:, t * 128:(t + 1) * 128] = xfin[p, r:r + 1, :]
    for p in range(4):
        out_c[:, p * 128:(p + 1) * 128] = xfin[p, 2:4, :]
    for copy in copies:
        copy.wait_send()


COPIES = 58


def shards(b, f, d, cf, e, idx, owner):
    vm = pltpu.VMEM
    any_spec = pl.BlockSpec(memory_space=pl.ANY)
    vmem_spec = pl.BlockSpec(memory_space=pltpu.VMEM)
    return pl.pallas_call(
        kernel,
        out_shape=(jax.ShapeDtypeStruct((1, 768), F32), jax.ShapeDtypeStruct((2, 512), F32)),
        in_specs=[any_spec] * 6 + [pl.BlockSpec(memory_space=pltpu.SMEM)],
        out_specs=(vmem_spec, vmem_spec),
        scratch_shapes=[
            vm((384, 1536), F32), vm((384, 768), F32), vm((192, 768), F32),
            vm((2, 256, 512), F32), vm((2, 512, 128), F32),
            vm((2, 256, 128), F32), vm((2, 256, 128), F32), vm((2, 1024, 128), F32),
            vm((4, 768, 128), F32), vm((4, 1536, 128), F32), vm((8, 1024), jnp.int32),
            vm((384, 256), F32),
            vm((2, 768, 1024), BF16), vm((2, 384, 1024), BF16),
            vm((384, 1536), BF16), vm((384, 1536), BF16),
            vm((384, 768), BF16), vm((384, 768), BF16),
            vm((192, 768), BF16), vm((192, 768), BF16),
            vm((2, 256, 512), BF16), vm((2, 256, 512), BF16),
            vm((2, 512, 128), BF16), vm((2, 512, 128), BF16),
            vm((2, 1024, 128), BF16), vm((2, 1024, 128), BF16),
            vm((768, 256), BF16), vm((768, 256), BF16),
            vm((768, 256), BF16), vm((768, 256), BF16),
            vm((1536, 256), BF16), vm((1536, 256), BF16),
            vm((8, 128), F32), vm((2, 4, 8, 128), F32), vm((8, 128), F32), vm((4, 8, 128), F32),
            pltpu.SemaphoreType.DMA((COPIES,)),
            pltpu.SemaphoreType.DMA((COPIES,)),
            pltpu.SemaphoreType.DMA((6,)),
        ],
        compiler_params=pltpu.CompilerParams(
            collective_id=0, has_side_effects=True, vmem_limit_bytes=60 * 1024 * 1024
        ),
        name="selected",
    )(b[0], f[0], d[0], cf, e, idx, owner)


def solution(mesh):
    split_spec = P("leaf", "front", None)
    in_specs = (split_spec,) * 5 + (P(), P())
    out_specs = (P("leaf", None), P("leaf", None))
    return jax.shard_map(shards, mesh=mesh, in_specs=in_specs, out_specs=out_specs, check_vma=False)
```

```python
import jax
import jax.numpy as jnp
from jax import lax
from jax.experimental import pallas as pl
from jax.experimental.pallas import tpu as pltpu
from jax.sharding import PartitionSpec as P

F32 = jnp.float32
BF16 = jnp.bfloat16
MESH = pl.DeviceIdType.MESH


def dot(a, b):
    return jnp.dot(a, b, preferred_element_type=F32)


def dot3(ah, al, bh, bl):
    return dot(ah, bh) + (dot(ah, bl) + dot(al, bh))


def split(x):
    hi = x.astype(BF16)
    return hi, (x - hi.astype(F32)).astype(BF16)


def col_sum(x):
    return jnp.sum(x, axis=0, keepdims=True)


def select(flag, yes, no):
    return jnp.where(jnp.full(yes.shape, flag, jnp.int32) == 1, yes, no)


def kernel(
    b_in, f_in, d_in, cf_in, e_in, idx_in, owner_in,
    out,
    b_s, f_s, d_s, cf_s, e_s, dp_s, k_own, k_par, k_s, v_s, v_pack, r_s, w_half, w_pack,
    idx_s, l_s, acc, owner,
    su, sl, bh, bl, fh, fl, dh, dl, ch, cl, eh, el, kh, kl, uh, ul, vh, vl, rh, rl,
    stage, fin, ostage, xfin, send, recv, loc,
):
    leaf = lax.axis_index("leaf")
    front = lax.axis_index("front")
    y = lax.div(front, 4)
    x = lax.rem(front, 4)
    partner = leaf + 1 - 2 * lax.rem(leaf, 2)
    copies = []

    def remote(src, dst, device):
        k = len(copies)
        copy = pltpu.make_async_remote_copy(
            src_ref=src, dst_ref=dst, send_sem=send.at[k], recv_sem=recv.at[k],
            device_id=device, device_id_type=MESH,
        )
        copies.append(copy)
        return copy

    def at_x(p):
        return {"front": y * 4 + p}

    def at_y(p):
        return {"front": p * 4 + x}

    class Ring:
        def __init__(self, device, pos, part, src=None):
            right, left = lax.rem(pos + 1, 4), lax.rem(pos + 3, 4)
            src = src or (lambda h: part(pos, h))
            self.right = [remote(src(h), part(pos, h), device(right)) for h in (0, 1)]
            self.left = [remote(src(h), part(pos, h), device(left)) for h in (1, 0)]
            self.next_right = remote(part(left, 0), part(left, 0), device(right))
            self.next_left = remote(part(right, 1), part(right, 1), device(left))

        def begin(self):
            for h in range(2):
                self.right[h].start()
                self.left[h].start()

        def relay(self):
            self.right[0].wait_recv()
            self.next_right.start()
            self.left[0].wait_recv()
            self.next_left.start()

        def near(self):
            self.right[1].wait_recv()
            self.left[1].wait_recv()

        def far(self):
            self.next_right.wait_recv()
            self.next_left.wait_recv()

        def finish(self):
            self.near()
            self.far()

    def halves(ref, size, *lead):
        return lambda p, h: ref.at[(*lead, pl.ds(p * size + h * (size // 2), size // 2), slice(None))]

    def of(ref, size):
        return lambda h: ref.at[pl.ds(h * (size // 2), size // 2), :]

    barrier = pltpu.get_barrier_semaphore()
    peers = [at_x(lax.rem(x + d, 4)) for d in (1, 2, 3)]
    peers += [at_y(lax.rem(y + d, 4)) for d in (1, 2, 3)]
    peers += [
        {"leaf": partner, "front": lax.rem(y + d, 4) * 4 + x} for d in (0, 1, 2, 3)
    ]
    for peer in peers:
        pl.semaphore_signal(barrier, inc=1, device_id=peer, device_id_type=MESH)

    def lanes(t):
        return pl.ds(pl.multiple_of(t * 128, 128), 128)

    def tiles(p):
        return lanes(p + lax.div(p + 1, 2)), lanes(1 + 3 * lax.div(p, 2))

    full_tile, half_tile = tiles(x)
    moves = [
        (idx_in.at[pl.ds(pl.multiple_of(lax.div(leaf, 4) * 8, 8), 8), :], idx_s),
        (owner_in, owner),
        (e_in.at[:, :, lanes(x)], e_s.at[:, pl.ds(y * 128 + x * 32, 32), :]),
        (d_in.at[:, full_tile], dp_s.at[0, pl.ds(x * 48, 48), :]),
        (d_in.at[:, half_tile], dp_s.at[1, pl.ds(x * 48, 48), :]),
        (cf_in, cf_s.at[:, pl.ds(x * 64, 64), :]),
        (d_in, d_s.at[pl.ds(x * 48, 48), :]),
        (f_in, f_s.at[pl.ds(x * 96, 96), :]),
        (b_in, b_s.at[pl.ds(x * 96, 96), :]),
    ]
    moves = [pltpu.make_async_copy(src, dst, loc.at[i]) for i, (src, dst) in enumerate(moves)]
    own_idx, own_owner, own_e, own_dp0, own_dp1, own_cf, own_d, own_f, own_b = moves
    for copy in moves:
        copy.start()

    e_across, d_across = [], []
    for d in (1, 3, 2):
        other = lax.rem(x + d, 4)
        e_across.append(remote(
            e_in.at[:, :, lanes(other)], e_s.at[:, pl.ds(y * 128 + x * 32, 32), :], at_x(other)
        ))
    for d in (1, 3, 2):
        other = lax.rem(x + d, 4)
        for t, tile in enumerate(tiles(other)):
            d_across.append(remote(
                d_in.at[:, tile], dp_s.at[t, pl.ds(x * 48, 48), :], at_x(other)
            ))
    ring_cf = Ring(at_x, x, lambda p, h: cf_s.at[h, pl.ds(p * 64, 64), :], lambda h: cf_in.at[h])
    ring_d = Ring(at_x, x, halves(d_s, 48), of(d_in, 48))
    ring_f = Ring(at_x, x, halves(f_s, 96), of(f_in, 96))
    ring_b = Ring(at_x, x, halves(b_s, 96), of(b_in, 96))
    ring_e = Ring(at_y, y, lambda p, h: e_s.at[h, pl.ds(p * 128, 128), :])
    ring_dp = Ring(at_y, y, halves(v_s, 192, 0))
    ring_dh = Ring(at_y, y, halves(v_pack, 96))
    ring_k = [Ring(at_y, y, halves(k_s, 256, c)) for c in range(2)]
    ring_v = [Ring(at_y, y, halves(v_s, 192, 1 + c)) for c in range(2)]
    ring_w = Ring(at_y, y, halves(r_s, 384, 0))
    ring_wh = Ring(at_y, y, halves(w_pack, 192))
    ring_r = [Ring(at_y, y, halves(r_s, 384, 1 + c)) for c in range(2)]
    k_cross = remote(k_own, k_par, {"leaf": partner})

    pl.semaphore_wait(barrier, 10)

    for copy in e_across + d_across:
        copy.start()
    ring_cf.begin()

    own_owner.wait()
    own_idx.wait()
    pool = (2 * leaf, 2 * leaf + 1, 2 * partner, 2 * partner + 1)
    mine = [(owner[p] == leaf).astype(jnp.int32) for p in pool]
    in_eight = [lax.rem(p, 8) for p in pool]

    def pick(c, items):
        if c == 0:
            return select(mine[0], items[0], select(mine[1], items[1], items[2]))
        return select(mine[3], items[3], select(mine[2], items[2], items[1]))

    idx_rows = [idx_s[pl.ds(p, 1), :] for p in in_eight]

    def one_hot(c):
        positions = pick(c, idx_rows)
        for m in range(0, 768, 128):
            at = lax.broadcasted_iota(jnp.int32, (128, 1024), 0) + m
            su[c, pl.ds(m, 128), :] = jnp.where(at == positions, 1.0, 0.0).astype(BF16)
        for m in range(0, 384, 128):
            at = lax.broadcasted_iota(jnp.int32, (128, 1024), 0) + (768 + 384 * y + m)
            sl[c, pl.ds(m, 128), :] = jnp.where(at == positions, 1.0, 0.0).astype(BF16)

    def split_rows(src, hi, lo, size, step):
        for m in range(0, size, step):
            h, l = split(src[pl.ds(m, step), :])
            hi[pl.ds(m, step), :] = h
            lo[pl.ds(m, step), :] = l

    def low_lanes(shape):
        return lax.broadcasted_iota(jnp.int32, shape, 1) < 64

    def pack(top, bottom):
        return jnp.where(low_lanes(top.shape), top, pltpu.roll(bottom, 64, 1))

    own_e.wait()
    for copy in e_across:
        copy.wait_recv()
    ring_e.begin()
    one_hot(0)

    own_dp0.wait()
    own_dp1.wait()
    for copy in d_across:
        copy.wait_recv()
    whole = dp_s[0]
    half = dp_s[1]
    half = select(lax.rem(x, 2), pltpu.roll(half, 64, 1), half)
    d_sums = [col_sum(whole * whole), col_sum(half * half)]
    v_s[0, pl.ds(pl.multiple_of(y * 192, 192), 192), :] = whole
    v_pack[pl.ds(pl.multiple_of(y * 96, 96), 96), :] = pack(half[:96], half[96:])
    ring_dp.begin()
    ring_dh.begin()
    ring_e.relay()
    ring_cf.relay()
    ring_d.begin()
    one_hot(1)
    ring_dp.relay()
    ring_dh.relay()

    ring_e.finish()
    e_sums = []
    for c in range(2):
        for m in range(0, 512, 128):
            h, l = split(e_s[c, pl.ds(m, 128), :])
            eh[c, pl.ds(m, 128), :] = h
            el[c, pl.ds(m, 128), :] = l
        part = e_s[c, pl.ds(pl.multiple_of(y * 128, 128), 128), :]
        e_sums.append(col_sum(part * part))
    own_cf.wait()
    ring_cf.finish()
    for c in range(2):
        for m in range(0, 256, 64):
            h, l = split(cf_s[c, pl.ds(m, 64), :])
            ch[c, pl.ds(m, 64), :] = h
            cl[c, pl.ds(m, 64), :] = l
        for m in range(0, 256, 128):
            at = pl.ds(m, 128)
            k_own[c, at, :] = dot3(ch[c, at, :], cl[c, at, :], eh[c], el[c])
    k_cross.start()
    ring_d.relay()
    ring_f.begin()
    k_cross.wait_recv()
    for c in range(2):
        for m in range(0, 256, 64):
            at = pl.ds(m, 64)
            pooled = [k_own[0, at, :], k_own[1, at, :], k_par[0, at, :], k_par[1, at, :]]
            k_s[c, pl.ds(pl.multiple_of(y * 256 + m, 64), 64), :] = pick(c, pooled)
        ring_k[c].begin()

    def split_to(value, hi, lo, row, col):
        h, l = split(value)
        hi[row, pl.ds(col, 128)] = h
        lo[row, pl.ds(col, 128)] = l

    ring_dp.finish()
    ring_dh.finish()
    for p in range(4):
        for m in (0, 96):
            split_to(v_s[0, pl.ds(192 * p + m, 96), :], vh, vl, pl.ds(192 * p + m, 96), 0)
            value = v_pack[pl.ds(96 * p, 96), :]
            if m:
                value = pltpu.roll(value, 64, 1)
            split_to(value, vh, vl, pl.ds(192 * p + m, 96), 128)
    ring_k[0].relay()
    own_d.wait()
    ring_d.finish()
    split_rows(d_s, dh, dl, 192, 48)
    ring_k[1].relay()
    ring_f.relay()
    ring_b.begin()

    v_sums = []
    for c in range(2):
        ring_k[c].finish()
        for m in range(0, 1024, 128):
            h, l = split(k_s[c, pl.ds(m, 128), :])
            kh[c, pl.ds(m, 128), :] = h
            kl[c, pl.ds(m, 128), :] = l
        for m in range(0, 768, 256):
            at = pl.ds(m, 256)
            uh[at, pl.ds(c * 128, 128)] = dot(su[c, at, :], kh[c]).astype(BF16)
            ul[at, pl.ds(c * 128, 128)] = dot(su[c, at, :], kl[c]).astype(BF16)
        cols = pl.ds(c * 128, 128)
        value = dot3(dh[...], dl[...], uh[:, cols], ul[:, cols])
        v_s[1 + c, pl.ds(pl.multiple_of(y * 192, 192), 192), :] = value
        v_sums.append(col_sum(value * value))
        ring_v[c].begin()

    ring_v[0].relay()
    own_f.wait()
    ring_f.finish()
    split_rows(f_s, fh, fl, 384, 48)
    ring_v[1].relay()
    parts = []
    for m in (0, 192):
        at = pl.ds(m, 192)
        value = dot3(fh[at, :], fl[at, :], vh[...], vl[...])
        r_s[0, pl.ds(pl.multiple_of(y * 384 + m, 192), 192), :] = value[:, :128]
        w_half[at, :] = value[:, 128:]
    ring_w.begin()
    w_pack[pl.ds(pl.multiple_of(y * 192, 192), 192), :] = pack(w_half[0:192, :], w_half[192:384, :])
    for c in range(2):
        for m in range(0, 384, 128):
            at = pl.ds(m, 128)
            l_s[at, pl.ds(c * 128, 128)] = dot(sl[c, at, :], kh[c]) + dot(sl[c, at, :], kl[c])

    for c in range(2):
        ring_v[c].finish()
        cols = pl.ds(c * 128, 128)
        for m in range(0, 768, 128):
            split_to(v_s[1 + c, pl.ds(m, 128), :], vh, vl, pl.ds(m, 128), 128 * c)
        for m in (0, 192):
            at = pl.ds(m, 192)
            value = l_s[at, cols] - dot3(fh[at, :], fl[at, :], vh[:, cols], vl[:, cols])
            r_s[1 + c, pl.ds(pl.multiple_of(y * 384 + m, 192), 192), :] = value
        ring_r[c].begin()
        if c == 0:
            ring_w.relay()
    ring_b.relay()
    ring_r[0].relay()
    ring_wh.begin()
    ring_w.finish()
    own_b.wait()
    ring_b.finish()
    split_rows(b_s, bh, bl, 384, 24)
    ring_r[1].relay()
    ring_wh.relay()

    ring_r[0].finish()
    for t in range(2):
        for m in range(0, 1536, 128):
            split_to(r_s[t, pl.ds(m, 128), :], rh, rl, pl.ds(m, 128), 128 * t)
    sums = [jnp.zeros((1, 128), F32)] * 4
    for m in range(0, 384, 128):
        at = pl.ds(m, 128)
        value = dot3(bh[at, :], bl[at, :], rh[...], rl[...])
        to = pl.ds(pl.multiple_of(y * 384 + m, 128), 128)
        for t in range(2):
            sums[t] = sums[t] + col_sum(value[:, t * 128:(t + 1) * 128] * r_s[t, to, :])

    def add_rows(p, first):
        for h in range(2):
            row = pl.ds(pl.multiple_of(p * 384 + h * 192, 192), 192)
            value = w_pack[pl.ds(pl.multiple_of(p * 192, 192), 192), :]
            if h:
                value = pltpu.roll(value, 64, 1)
            split_to(value, rh, rl, row, 0)
            split_to(r_s[2, row, :], rh, rl, row, 128)
        cols = pl.ds(pl.multiple_of(p * 384, 128), 384)
        row = pl.ds(pl.multiple_of(p * 384, 384), 384)
        for m in range(0, 384, 128):
            at = pl.ds(m, 128)
            value = dot3(bh[at, cols], bl[at, cols], rh[row, :], rl[row, :])
            acc[at, :] = value if first else acc[at, :] + value

    ring_wh.finish()
    add_rows(y, True)
    ring_r[1].near()
    add_rows(lax.rem(y + 1, 4), False)
    add_rows(lax.rem(y + 3, 4), False)
    ring_r[1].far()
    add_rows(lax.rem(y + 2, 4), False)
    for m in range(0, 384, 128):
        at = pl.ds(m, 128)
        to = pl.ds(pl.multiple_of(y * 384 + m, 128), 128)
        sums[2] = sums[2] + col_sum(acc[at, 0:128] * w_half[at, :])
        sums[3] = sums[3] + col_sum(acc[at, 128:256] * r_s[2, to, :])

    stage[0:1, :] = sums[0] + d_sums[0]
    stage[1:2, :] = sums[2] + d_sums[1]
    stage[2:3, :] = sums[1] + v_sums[0]
    stage[3:4, :] = sums[3] + v_sums[1]
    stage[4:5, :] = e_sums[0]
    stage[5:6, :] = e_sums[1]
    stage[6:8, :] = jnp.zeros((2, 128), F32)
    fin[0, y] = stage[...]
    ends = []
    for d in (1, 3, 2):
        ends.append(remote(stage, fin.at[0, y], at_y(lax.rem(y + d, 4))))
    for d in (0, 1, 3, 2):
        ends.append(remote(stage, fin.at[1, y], {"leaf": partner, "front": lax.rem(y + d, 4) * 4 + x}))
    for copy in ends:
        copy.start()
    for copy in ends:
        copy.wait_recv()
    own = ((fin[0, 0] + fin[0, 1]) + fin[0, 2]) + fin[0, 3]
    other = ((fin[1, 0] + fin[1, 1]) + fin[1, 2]) + fin[1, 3]
    before = 2 - mine[2] - mine[3]
    quad_0 = select(mine[0], own[2:3], select(before, other[3:4], other[2:3]))
    quad_1 = select(mine[1], select(mine[0], own[3:4], own[2:3]), other[3:4])
    ostage[0:2, :] = own[0:2]
    ostage[2:3, :] = own[4:5] + quad_0
    ostage[3:4, :] = own[5:6] + quad_1
    ostage[4:8, :] = jnp.zeros((4, 128), F32)
    xfin[x] = ostage[...]
    ends = []
    for d in (1, 3, 2):
        ends.append(remote(ostage, xfin.at[x], at_x(lax.rem(x + d, 4))))
    for copy in ends:
        copy.start()
    for copy in ends:
        copy.wait_recv()
    for p, t in enumerate((0, 2, 3, 5)):
        out[t:t + 1, :] = xfin[p, 0:1, :]
        out[8 + 2 * p:10 + 2 * p, :] = xfin[p, 2:4, :]
    for p, t in ((0, 1), (2, 4)):
        out[t:t + 1, :] = pack(xfin[p, 1:2, :], xfin[p + 1, 1:2, :])
    out[6:8, :] = jnp.zeros((2, 128), F32)
    for copy in copies:
        copy.wait_send()


COPIES = 110


def shards(b, f, d, cf, e, idx, owner):
    vm = pltpu.VMEM
    any_spec = pl.BlockSpec(memory_space=pl.ANY)
    vmem_spec = pl.BlockSpec(memory_space=pltpu.VMEM)
    out = pl.pallas_call(
        kernel,
        out_shape=jax.ShapeDtypeStruct((16, 128), F32),
        in_specs=[any_spec] * 7,
        out_specs=vmem_spec,
        scratch_shapes=[
            vm((384, 1536), F32), vm((384, 768), F32), vm((192, 768), F32),
            vm((2, 256, 512), F32), vm((2, 512, 128), F32), vm((2, 192, 128), F32),
            vm((2, 256, 128), F32), vm((2, 256, 128), F32), vm((2, 1024, 128), F32),
            vm((3, 768, 128), F32), vm((384, 128), F32),
            vm((3, 1536, 128), F32), vm((384, 128), F32), vm((768, 128), F32),
            vm((8, 1024), jnp.int32), vm((384, 256), F32), vm((384, 256), F32),
            pltpu.SMEM((64,), jnp.int32),
            vm((2, 768, 1024), BF16), vm((2, 384, 1024), BF16),
            vm((384, 1536), BF16), vm((384, 1536), BF16),
            vm((384, 768), BF16), vm((384, 768), BF16),
            vm((192, 768), BF16), vm((192, 768), BF16),
            vm((2, 256, 512), BF16), vm((2, 256, 512), BF16),
            vm((2, 512, 128), BF16), vm((2, 512, 128), BF16),
            vm((2, 1024, 128), BF16), vm((2, 1024, 128), BF16),
            vm((768, 256), BF16), vm((768, 256), BF16),
            vm((768, 256), BF16), vm((768, 256), BF16),
            vm((1536, 256), BF16), vm((1536, 256), BF16),
            vm((8, 128), F32), vm((2, 4, 8, 128), F32), vm((8, 128), F32), vm((4, 8, 128), F32),
            pltpu.SemaphoreType.DMA((COPIES,)),
            pltpu.SemaphoreType.DMA((COPIES,)),
            pltpu.SemaphoreType.DMA((9,)),
        ],
        compiler_params=pltpu.CompilerParams(
            collective_id=0, has_side_effects=True, vmem_limit_bytes=60 * 1024 * 1024
        ),
        name="selected",
    )(b[0], f[0], d[0], cf, e, idx, owner)
    kids = out[8:16].reshape(4, 2, 128).transpose(1, 0, 2).reshape(2, 512)
    return out[0:6].reshape(1, 768), kids


def solution(mesh):
    split_spec = P("leaf", "front", None)
    in_specs = (split_spec,) * 5 + (P(), P())
    out_specs = (P("leaf", None), P("leaf", None))
    return jax.shard_map(shards, mesh=mesh, in_specs=in_specs, out_specs=out_specs, check_vma=False)
```

```python
import jax
import jax.numpy as jnp
from jax import lax
from jax.experimental import pallas as pl
from jax.experimental.pallas import tpu as pltpu
from jax.sharding import PartitionSpec as P

F32 = jnp.float32
BF16 = jnp.bfloat16
MESH = pl.DeviceIdType.MESH


def dot(a, b):
    return jnp.dot(a, b, preferred_element_type=F32)


def dot3(ah, al, bh, bl):
    return dot(ah, bh) + (dot(ah, bl) + dot(al, bh))


def split(x):
    hi = x.astype(BF16)
    return hi, (x - hi.astype(F32)).astype(BF16)


def col_sum(x):
    return jnp.sum(x, axis=0, keepdims=True)


def select(flag, yes, no):
    return jnp.where(jnp.full(yes.shape, flag, jnp.int32) == 1, yes, no)


def kernel(
    b_in, f_in, d_in, cf_in, e_in, idx_in, owner_in,
    out,
    e_raw, c_raw, e_sel, c_sel,
    b_s, f_s, d_s, cf_s, e_s, dp_s, k_s, v_s, v_pack, r_s, w_half, w_pack, w_tile, w_side,
    idx_s, l_s, acc, owner,
    su, sl, bh, bl, fh, fl, dh, dl, ch, cl, eh, el, kh, kl, uh, ul, vh, vl, wh, wl, rh, rl,
    stage, fin, ostage, xfin, send, recv, loc,
):
    leaf = lax.axis_index("leaf")
    front = lax.axis_index("front")
    y = lax.div(front, 4)
    x = lax.rem(front, 4)
    core = lax.rem(leaf, 2)
    base = leaf - core
    partner = base + 1 - core
    group = lax.div(x, 2)
    pair = x + 1 - 2 * lax.rem(x, 2)
    col = 2 * lax.rem(x, 2) + core
    hub = core == group
    copies, hub_copies, kept_copies = [], [], []
    taken = [0, 0]

    def remote(src, dst, device, group_of=None, at=None):
        if at is None:
            at = taken[1]
            taken[1] += 1
        copy = pltpu.make_async_remote_copy(
            src_ref=src, dst_ref=dst, send_sem=send.at[taken[0]], recv_sem=recv.at[at],
            device_id=device, device_id_type=MESH,
        )
        taken[0] += 1
        (copies if group_of is None else group_of).append(copy)
        return copy

    def slots(n):
        taken[1] += n
        return taken[1] - n

    def at_y(p):
        return {"front": p * 4 + x}

    def on(chip, a_core=None):
        if a_core is None:
            return {"front": y * 4 + chip}
        return {"leaf": base + a_core, "front": y * 4 + chip}

    other_core = {"leaf": partner}

    class Ring:
        def __init__(self, part):
            right, left = lax.rem(y + 1, 4), lax.rem(y + 3, 4)
            self.right = [remote(part(y, h), part(y, h), at_y(right)) for h in (0, 1)]
            self.left = [remote(part(y, h), part(y, h), at_y(left)) for h in (1, 0)]
            self.next_right = remote(part(left, 0), part(left, 0), at_y(right))
            self.next_left = remote(part(right, 1), part(right, 1), at_y(left))

        def begin(self):
            for h in range(2):
                self.right[h].start()
                self.left[h].start()

        def relay(self):
            self.right[0].wait_recv()
            self.next_right.start()
            self.left[0].wait_recv()
            self.next_left.start()

        def near(self):
            self.right[1].wait_recv()
            self.left[1].wait_recv()

        def far(self):
            self.next_right.wait_recv()
            self.next_left.wait_recv()

        def finish(self):
            self.near()
            self.far()

    class Rows:
        def __init__(self, part, whole, src, local):
            first = slots(4)
            role = jnp.where(hub, 0, 2)
            goal = jnp.where(hub, pair, 3 - x)
            self.first = [remote(src(h), part(x, h), on(goal), at=first + role + h) for h in (0, 1)]
            self.pair_in = [
                pltpu.make_async_remote_copy(
                    src_ref=part(pair, h), dst_ref=part(pair, h), send_sem=send.at[0],
                    recv_sem=recv.at[first + h], device_id=on(pair), device_id_type=MESH,
                ) for h in (0, 1)
            ]
            self.far_in = [
                pltpu.make_async_remote_copy(
                    src_ref=part(3 - x, h), dst_ref=part(3 - x, h), send_sem=send.at[0],
                    recv_sem=recv.at[first + 2 + h], device_id=on(pair), device_id_type=MESH,
                ) for h in (0, 1)
            ]
            self.next = [
                remote(part(3 - x, h), part(3 - x, h), on(pair), hub_copies) for h in (0, 1)
            ]
            self.inside = [
                remote(whole(p), whole(p), other_core, hub_copies) for p in (x, 3 - x, pair, 3 - pair)
            ]
            self.own, self.whole = local, whole

        def keep(self, sem):
            self.local = pltpu.make_async_copy(self.own, self.whole(x), loc.at[sem])

            @pl.when(hub)
            def _():
                self.local.start()

        def begin(self):
            for h in range(2):
                self.first[h].start()

        def relay(self):
            @pl.when(hub)
            def _():
                self.local.wait()
                self.inside[0].start()
                for h in range(2):
                    self.far_in[h].wait_recv()
                    self.next[h].start()
                self.inside[1].start()

        def near(self):
            @pl.when(hub)
            def _():
                for h in range(2):
                    self.pair_in[h].wait_recv()
                self.inside[2].start()

        def finish(self):
            @pl.when(hub)
            def _():
                for h in range(2):
                    self.next[h].wait_recv()
                self.inside[3].start()

            @pl.when(jnp.logical_not(hub))
            def _():
                for copy in self.inside:
                    copy.wait_recv()

    def halves(ref, size, *lead):
        return lambda p, h: ref.at[(*lead, pl.ds(p * size + h * (size // 2), size // 2), slice(None))]

    def wholes(ref, size):
        return lambda p: ref.at[pl.ds(p * size, size), :]

    def of(ref, size):
        return lambda h: ref.at[pl.ds(h * (size // 2), size // 2), :]

    barrier = pltpu.get_barrier_semaphore()
    peers = [at_y(lax.rem(y + d, 4)) for d in (1, 2, 3)]
    row_peers = [on(lax.rem(x + d, 4), core) for d in (1, 3, 2)]
    row_peers += [on(lax.rem(x + d, 4), 1 - core) for d in (0, 1, 3, 2)]
    for peer in peers + row_peers:
        pl.semaphore_signal(barrier, inc=1, device_id=peer, device_id_type=MESH)

    def lanes(t):
        return pl.ds(pl.multiple_of(t * 128, 128), 128)

    def tiles(p):
        return lanes(p + lax.div(p + 1, 2)), lanes(1 + 3 * lax.div(p, 2))

    full_tile, half_tile = tiles(col)
    moves = [
        (idx_in.at[pl.ds(pl.multiple_of(lax.div(leaf, 4) * 8, 8), 8), :], idx_s),
        (owner_in, owner),
        (e_in, e_raw.at[0]),
        (cf_in, c_raw.at[0]),
    ]
    moves = [pltpu.make_async_copy(src, dst, loc.at[i]) for i, (src, dst) in enumerate(moves)]
    own_idx, own_owner, own_e, own_cf = moves
    for copy in (own_owner, own_e, own_cf, own_idx):
        copy.start()

    e_cross = remote(e_in, e_raw.at[1], other_core)
    c_cross = remote(cf_in, c_raw.at[1], other_core)

    e_rows = lambda p: e_s.at[:, pl.ds(y * 128 + p * 32, 32), :]
    d_rows = lambda t, p: dp_s.at[t, pl.ds(p * 48, 48), :]
    e_at, d_at = slots(4), slots(8)
    e_across, d_across, is_own = [], [], []
    for j in range(4):
        goal = on(2 * core + j // 2, j % 2)
        is_own.append(jnp.logical_and(hub, col == j))
        e_across.append([remote(e_sel.at[:, :, lanes(j)], e_rows(x), goal, kept_copies, e_at + x)])
        d_across.append([
            remote(d_in.at[:, tile], d_rows(t, x), goal, kept_copies, d_at + 2 * x + t)
            for t, tile in enumerate(tiles(jnp.int32(j)))
        ])

    def arriving(dst, at):
        return pltpu.make_async_remote_copy(
            src_ref=dst, dst_ref=dst, send_sem=send.at[0], recv_sem=recv.at[at],
            device_id=on(pair), device_id_type=MESH,
        )

    e_kept = [pltpu.make_async_copy(e_sel.at[:, :, lanes(col)], e_rows(x), loc.at[4])]
    d_kept = [
        pltpu.make_async_copy(d_in.at[:, full_tile], d_rows(0, x), loc.at[5]),
        pltpu.make_async_copy(d_in.at[:, half_tile], d_rows(1, x), loc.at[6]),
    ]

    def scatter(across, kept):
        @pl.when(hub)
        def _():
            for copy in kept:
                copy.start()

        for j in range(4):
            @pl.when(jnp.logical_not(is_own[j]))
            def _(j=j):
                for copy in across[j]:
                    copy.start()

    def gather(kept, pieces):
        @pl.when(hub)
        def _():
            for copy in kept:
                copy.wait()

        for p in range(4):
            @pl.when(jnp.logical_not(jnp.logical_and(hub, x == p)))
            def _(p=p):
                for copy in pieces(p):
                    copy.wait_recv()

    rows_c = Rows(
        lambda p, h: cf_s.at[h, pl.ds(p * 64, 64), :], lambda p: cf_s.at[:, pl.ds(p * 64, 64), :],
        lambda h: c_sel.at[h], c_sel,
    )
    rows_f = Rows(halves(f_s, 96), wholes(f_s, 96), of(f_in, 96), f_in)
    rows_d = Rows(halves(d_s, 48), wholes(d_s, 48), of(d_in, 48), d_in)
    rows_b = Rows(halves(b_s, 96), wholes(b_s, 96), of(b_in, 96), b_in)
    ring_e = Ring(lambda p, h: e_s.at[h, pl.ds(p * 128, 128), :])
    ring_dp = Ring(halves(v_s, 192))
    ring_dh = Ring(halves(v_pack, 96))
    ring_k = [Ring(halves(k_s, 256, c)) for c in range(2)]
    ring_w = Ring(halves(r_s, 384, 0))
    ring_wh = Ring(halves(w_pack, 192))
    ring_r = [Ring(halves(r_s, 384, 1 + c)) for c in range(2)]
    w_pair, w_in, w_on = [], [], []
    for ref in (w_tile, w_side):
        w_pair.append(remote(ref.at[col], ref.at[col], on(pair)))
        w_in.append(remote(ref.at[col], ref.at[col], other_core))
    for ref in (w_tile, w_side):
        far_col = 2 * lax.rem(pair, 2) + core
        w_on.append(remote(ref.at[far_col], ref.at[far_col], other_core))

    rows_f.keep(7)
    rows_d.keep(8)
    rows_b.keep(9)

    pl.semaphore_wait(barrier, 10)

    e_cross.start()
    c_cross.start()
    scatter(d_across, d_kept)

    def members(mine_leaf, other_leaf):
        pool = (2 * mine_leaf, 2 * mine_leaf + 1, 2 * other_leaf, 2 * other_leaf + 1)
        return pool, [(owner[p] == mine_leaf).astype(jnp.int32) for p in pool]

    def pick(c, flags, items):
        if c == 0:
            return select(flags[0], items[0], select(flags[1], items[1], items[2]))
        return select(flags[3], items[3], select(flags[2], items[2], items[1]))

    own_owner.wait()
    _, mine = members(leaf, partner)
    pool, held = members(base + group, base + 1 - group)
    own_e.wait()
    e_cross.wait_recv()
    for c in range(2):
        e_sel[c] = pick(c, mine, [e_raw[0, 0], e_raw[0, 1], e_raw[1, 0], e_raw[1, 1]])
    scatter(e_across, e_kept)
    own_cf.wait()
    c_cross.wait_recv()
    for c in range(2):
        for m in (0, 32):
            at = pl.ds(m, 32)
            c_sel[c, at, :] = pick(
                c, mine, [c_raw[0, 0, at, :], c_raw[0, 1, at, :], c_raw[1, 0, at, :], c_raw[1, 1, at, :]]
            )
    rows_c.begin()
    rows_c.keep(10)

    own_idx.wait()
    idx_rows = [idx_s[pl.ds(lax.rem(p, 8), 1), :] for p in pool]

    def one_hot(c):
        positions = pick(c, held, idx_rows)
        for m in range(0, 768, 128):
            at = lax.broadcasted_iota(jnp.int32, (128, 1024), 0) + m
            su[c, pl.ds(m, 128), :] = jnp.where(at == positions, 1.0, 0.0).astype(BF16)
        for m in range(0, 384, 128):
            at = lax.broadcasted_iota(jnp.int32, (128, 1024), 0) + (768 + 384 * y + m)
            sl[c, pl.ds(m, 128), :] = jnp.where(at == positions, 1.0, 0.0).astype(BF16)

    def split_rows(src, hi, lo, size, step):
        for m in range(0, size, step):
            h, l = split(src[pl.ds(m, step), :])
            hi[pl.ds(m, step), :] = h
            lo[pl.ds(m, step), :] = l

    def split_to(value, hi, lo, row, lane):
        h, l = split(value)
        hi[row, pl.ds(lane, 128)] = h
        lo[row, pl.ds(lane, 128)] = l

    def low_lanes(shape):
        return lax.broadcasted_iota(jnp.int32, shape, 1) < 64

    def swap(value):
        return pltpu.roll(value, 64, 1)

    def pack(top, bottom):
        return jnp.where(low_lanes(top.shape), top, swap(bottom))

    gather(d_kept, lambda p: [arriving(d_rows(t, p), d_at + 2 * p + t) for t in range(2)])
    whole = dp_s[0]
    half = select(core, swap(dp_s[1]), dp_s[1])
    d_sums = [col_sum(whole * whole), col_sum(half * half)]
    v_s[pl.ds(pl.multiple_of(y * 192, 192), 192), :] = whole
    v_pack[pl.ds(pl.multiple_of(y * 96, 96), 96), :] = pack(half[:96], half[96:])
    ring_dp.begin()
    ring_dh.begin()
    gather(e_kept, lambda p: [arriving(e_rows(p), e_at + p)])
    ring_e.begin()
    rows_c.relay()
    rows_f.begin()
    one_hot(0)
    ring_dp.relay()
    ring_dh.relay()
    rows_c.near()
    ring_e.relay()

    ring_e.finish()
    e_sums = []
    for c in range(2):
        for m in range(0, 512, 128):
            h, l = split(e_s[c, pl.ds(m, 128), :])
            eh[c, pl.ds(m, 128), :] = h
            el[c, pl.ds(m, 128), :] = l
        part = e_s[c, pl.ds(pl.multiple_of(y * 128, 128), 128), :]
        e_sums.append(col_sum(part * part))
    rows_c.finish()
    for c in range(2):
        for m in range(0, 256, 64):
            h, l = split(cf_s[c, pl.ds(m, 64), :])
            ch[c, pl.ds(m, 64), :] = h
            cl[c, pl.ds(m, 64), :] = l
        for m in range(0, 256, 128):
            at = pl.ds(m, 128)
            k_s[c, pl.ds(pl.multiple_of(y * 256 + m, 128), 128), :] = dot3(ch[c, at, :], cl[c, at, :], eh[c], el[c])
        ring_k[c].begin()
    rows_f.relay()
    rows_d.begin()
    one_hot(1)
    rows_f.near()

    ring_dp.finish()
    ring_dh.finish()
    for p in range(4):
        for m in (0, 96):
            split_to(v_s[pl.ds(192 * p + m, 96), :], vh, vl, pl.ds(192 * p + m, 96), 0)
            value = v_pack[pl.ds(96 * p, 96), :]
            split_to(swap(value) if m else value, vh, vl, pl.ds(192 * p + m, 96), 128)
    ring_k[0].relay()
    rows_f.finish()
    split_rows(f_s, fh, fl, 384, 48)
    for m in (0, 192):
        at = pl.ds(m, 192)
        value = dot3(fh[at, :], fl[at, :], vh[...], vl[...])
        r_s[0, pl.ds(pl.multiple_of(y * 384 + m, 192), 192), :] = value[:, :128]
        w_tile[col, at, :] = value[:, :128]
        w_half[at, :] = value[:, 128:]
    packed = pack(w_half[0:192, :], w_half[192:384, :])
    w_pack[pl.ds(pl.multiple_of(y * 192, 192), 192), :] = packed
    w_side[col] = packed
    for copy in w_pair + w_in:
        copy.start()
    ring_k[1].relay()
    ring_w.begin()
    rows_d.relay()
    rows_b.begin()
    rows_d.near()

    for c in range(2):
        ring_k[c].finish()
        for m in range(0, 1024, 128):
            h, l = split(k_s[c, pl.ds(m, 128), :])
            kh[c, pl.ds(m, 128), :] = h
            kl[c, pl.ds(m, 128), :] = l
        for m in range(0, 768, 256):
            at = pl.ds(m, 256)
            uh[at, pl.ds(c * 128, 128)] = dot(su[c, at, :], kh[c]).astype(BF16)
            ul[at, pl.ds(c * 128, 128)] = dot(su[c, at, :], kl[c]).astype(BF16)
        if c == 0:
            ring_w.relay()
            ring_wh.begin()
        for m in range(0, 384, 128):
            at = pl.ds(m, 128)
            l_s[at, pl.ds(c * 128, 128)] = dot(sl[c, at, :], kh[c]) + dot(sl[c, at, :], kl[c])

    for copy in w_pair:
        copy.wait_recv()
    for copy in w_on:
        copy.start()
    rows_d.finish()
    for copy in w_in + w_on:
        copy.wait_recv()
    for p, t in enumerate((0, 2, 3, 5)):
        for m in (0, 192):
            split_to(w_tile[p, pl.ds(m, 192), :], wh, wl, pl.ds(m, 192), 128 * t)
    for p, t in ((0, 1), (2, 4)):
        low, high = w_side[p], w_side[p + 1]
        split_to(jnp.where(low_lanes(low.shape), low, swap(high)), wh, wl, pl.ds(0, 192), 128 * t)
        split_to(jnp.where(low_lanes(low.shape), swap(low), high), wh, wl, pl.ds(192, 192), 128 * t)
    for c in range(2):
        cols = pl.ds(c * 128, 128)
        for m in (0, 192):
            at = pl.ds(m, 192)
            value = l_s[at, cols] - dot3(wh[at, :], wl[at, :], uh[:, cols], ul[:, cols])
            r_s[1 + c, pl.ds(pl.multiple_of(y * 384 + m, 192), 192), :] = value
        ring_r[c].begin()
    ring_wh.relay()
    rows_b.relay()
    rows_b.near()
    split_rows(d_s, dh, dl, 192, 48)
    value = dot3(dh[...], dl[...], uh[...], ul[...])
    v_sums = col_sum(value * value)
    ring_r[0].relay()
    ring_r[1].relay()
    ring_w.finish()
    ring_wh.finish()
    rows_b.finish()
    split_rows(b_s, bh, bl, 384, 24)

    def split_half(p):
        value = w_pack[pl.ds(pl.multiple_of(p * 192, 192), 192), :]
        split_to(value, rh, rl, pl.ds(pl.multiple_of(p * 384, 192), 192), 128)
        split_to(swap(value), rh, rl, pl.ds(pl.multiple_of(p * 384 + 192, 192), 192), 128)

    for p in range(4):
        split_half(p)
    for m in range(0, 1536, 128):
        split_to(r_s[0, pl.ds(m, 128), :], rh, rl, pl.ds(m, 128), 0)
    p_sums = list(d_sums)
    for m in range(0, 384, 128):
        at = pl.ds(m, 128)
        value = dot3(bh[at, :], bl[at, :], rh[...], rl[...])
        to = pl.ds(pl.multiple_of(y * 384 + m, 128), 128)
        p_sums[0] = p_sums[0] + col_sum(value[:, :128] * r_s[0, to, :])
        p_sums[1] = p_sums[1] + col_sum(value[:, 128:] * w_half[at, :])

    def add_rows(p, first):
        row = pl.ds(pl.multiple_of(p * 384, 384), 384)
        for c in range(2):
            split_to(r_s[1 + c, row, :], rh, rl, row, 128 * c)
        cols = pl.ds(pl.multiple_of(p * 384, 128), 384)
        for m in range(0, 384, 128):
            at = pl.ds(m, 128)
            value = dot3(bh[at, cols], bl[at, cols], rh[row, :], rl[row, :])
            acc[at, :] = value if first else acc[at, :] + value

    add_rows(y, True)
    for c in range(2):
        ring_r[c].near()
    add_rows(lax.rem(y + 1, 4), False)
    add_rows(lax.rem(y + 3, 4), False)
    for c in range(2):
        ring_r[c].far()
    add_rows(lax.rem(y + 2, 4), False)
    c_sums = [e_sums[c] + v_sums[:, c * 128:(c + 1) * 128] for c in range(2)]
    for m in range(0, 384, 128):
        to = pl.ds(pl.multiple_of(y * 384 + m, 128), 128)
        for c in range(2):
            c_sums[c] = c_sums[c] + col_sum(acc[pl.ds(m, 128), c * 128:(c + 1) * 128] * r_s[1 + c, to, :])

    for c in range(2):
        stage[c:c + 1, :] = p_sums[c]
        stage[2 + c:3 + c, :] = c_sums[c]
    stage[4:8, :] = jnp.zeros((4, 128), F32)
    fin[y] = stage[...]
    ends = [remote(stage, fin.at[y], at_y(lax.rem(y + d, 4))) for d in (1, 3, 2)]
    for copy in ends:
        copy.start()
    for copy in ends:
        copy.wait_recv()
    ostage[...] = ((fin[0] + fin[1]) + fin[2]) + fin[3]
    place = 4 * group + col
    xfin[place] = ostage[...]
    ends = [remote(ostage, xfin.at[place], peer) for peer in row_peers]
    for copy in ends:
        copy.start()
    for copy in ends:
        copy.wait_recv()
    before = 2 - mine[2] - mine[3]
    for j in range(4):
        own, other = xfin[4 * core + j], xfin[4 - 4 * core + j]
        out[8 + 2 * j:9 + 2 * j, :] = select(mine[0], own[2:3], select(before, other[3:4], other[2:3]))
        out[9 + 2 * j:10 + 2 * j, :] = select(mine[1], select(mine[0], own[3:4], own[2:3]), other[3:4])
        t = (0, 2, 3, 5)[j]
        out[t:t + 1, :] = own[0:1]
        if j in (0, 2):
            after = xfin[4 * core + j + 1]
            out[t + 1:t + 2, :] = pack(own[1:2], after[1:2])
    out[6:8, :] = jnp.zeros((2, 128), F32)
    for copy in copies:
        copy.wait_send()

    @pl.when(hub)
    def _():
        for copy in hub_copies:
            copy.wait_send()

    for j in range(4):
        @pl.when(jnp.logical_not(is_own[j]))
        def _(j=j):
            for copy in e_across[j] + d_across[j]:
                copy.wait_send()


COPIES = 160


def shards(b, f, d, cf, e, idx, owner):
    vm = pltpu.VMEM
    any_spec = pl.BlockSpec(memory_space=pl.ANY)
    vmem_spec = pl.BlockSpec(memory_space=pltpu.VMEM)
    out = pl.pallas_call(
        kernel,
        out_shape=jax.ShapeDtypeStruct((16, 128), F32),
        in_specs=[any_spec] * 7,
        out_specs=vmem_spec,
        scratch_shapes=[
            vm((2, 2, 32, 512), F32), vm((2, 2, 64, 512), F32), vm((2, 32, 512), F32), vm((2, 64, 512), F32),
            vm((384, 1536), F32), vm((384, 768), F32), vm((192, 768), F32),
            vm((2, 256, 512), F32), vm((2, 512, 128), F32), vm((2, 192, 128), F32),
            vm((2, 1024, 128), F32), vm((768, 128), F32), vm((384, 128), F32),
            vm((3, 1536, 128), F32), vm((384, 128), F32), vm((768, 128), F32),
            vm((4, 384, 128), F32), vm((4, 192, 128), F32),
            vm((8, 1024), jnp.int32), vm((384, 256), F32), vm((384, 256), F32),
            pltpu.SMEM((64,), jnp.int32),
            vm((2, 768, 1024), BF16), vm((2, 384, 1024), BF16),
            vm((384, 1536), BF16), vm((384, 1536), BF16),
            vm((384, 768), BF16), vm((384, 768), BF16),
            vm((192, 768), BF16), vm((192, 768), BF16),
            vm((2, 256, 512), BF16), vm((2, 256, 512), BF16),
            vm((2, 512, 128), BF16), vm((2, 512, 128), BF16),
            vm((2, 1024, 128), BF16), vm((2, 1024, 128), BF16),
            vm((768, 256), BF16), vm((768, 256), BF16),
            vm((768, 256), BF16), vm((768, 256), BF16),
            vm((384, 768), BF16), vm((384, 768), BF16),
            vm((1536, 256), BF16), vm((1536, 256), BF16),
            vm((8, 128), F32), vm((4, 8, 128), F32), vm((8, 128), F32), vm((8, 8, 128), F32),
            pltpu.SemaphoreType.DMA((COPIES,)),
            pltpu.SemaphoreType.DMA((COPIES,)),
            pltpu.SemaphoreType.DMA((11,)),
        ],
        compiler_params=pltpu.CompilerParams(
            collective_id=0, has_side_effects=True, vmem_limit_bytes=60 * 1024 * 1024
        ),
        name="selected",
    )(b[0], f[0], d[0], cf, e, idx, owner)
    kids = out[8:16].reshape(4, 2, 128).transpose(1, 0, 2).reshape(2, 512)
    return out[0:6].reshape(1, 768), kids


def solution(mesh):
    split_spec = P("leaf", "front", None)
    in_specs = (split_spec,) * 5 + (P(), P())
    out_specs = (P("leaf", None), P("leaf", None))
    return jax.shard_map(shards, mesh=mesh, in_specs=in_specs, out_specs=out_specs, check_vma=False)
```

```python
import jax
import jax.numpy as jnp
from jax import lax
from jax.experimental import pallas as pl
from jax.experimental.pallas import tpu as pltpu
from jax.sharding import PartitionSpec as P

F32 = jnp.float32
BF16 = jnp.bfloat16
MESH = pl.DeviceIdType.MESH


def dot(a, b):
    return jnp.dot(a, b, preferred_element_type=F32)


def dot3(ah, al, bh, bl):
    return dot(ah, bh) + (dot(ah, bl) + dot(al, bh))


def split(x):
    hi = x.astype(BF16)
    return hi, (x - hi.astype(F32)).astype(BF16)


def col_sum(x):
    return jnp.sum(x, axis=0, keepdims=True)


def select(flag, yes, no):
    return jnp.where(jnp.full(yes.shape, flag, jnp.int32) == 1, yes, no)


def kernel(
    b_in, f_in, d_in, cf_in, e_in, idx_in, owner_in,
    out_p, out_d, out_c, out_e,
    e_raw, c_raw, e_sel, c_sel,
    b_s, f_s, d_s, cf_s, e_s, k_s, v_s, r_s, w_half, w_s, w_x,
    idx_s, l_s, acc, owner,
    su, sl, bh, bl, fh, fl, dh, dl, ch, cl, eh, el, kh, kl, uh, ul, vh, vl, wh, wl, rh, rl,
    stage, fin, ostage, xfin, send, recv, loc,
):
    leaf = lax.axis_index("leaf")
    front = lax.axis_index("front")
    y = lax.div(front, 4)
    x = lax.rem(front, 4)
    core = lax.rem(leaf, 2)
    base = leaf - core
    partner = base + 1 - core
    group = lax.div(x, 2)
    pair = x + 1 - 2 * lax.rem(x, 2)
    col = 2 * lax.rem(x, 2) + core
    hub = core == group
    taken = [0, 0]

    def sends():
        taken[0] += 1
        return send.at[taken[0] - 1]

    def arrivals(n=1):
        taken[1] += n
        return recv.at[taken[1] - 1] if n == 1 else taken[1] - n

    def remote(src, dst, device, sent, arrived):
        return pltpu.make_async_remote_copy(
            src_ref=src, dst_ref=dst, send_sem=sent, recv_sem=arrived,
            device_id=device, device_id_type=MESH,
        )

    def wait(ref, sem):
        pltpu.make_async_copy(ref, ref, sem).wait()

    def at_y(p):
        return {"front": p * 4 + x}

    def on(chip, a_core=None):
        if a_core is None:
            return {"front": y * 4 + chip}
        return {"leaf": base + a_core, "front": y * 4 + chip}

    other_core = {"leaf": partner}

    rings, matrices = [], []

    class Ring:
        def __init__(self, part, span):
            right, left = lax.rem(y + 1, 4), lax.rem(y + 3, 4)
            self.span, self.sent = span, sends()
            self.near_sem, self.far_sem = arrivals(), arrivals()
            self.right = [
                remote(part(y, h), part(y, h), at_y(right), self.sent, at)
                for h, at in ((0, arrivals()), (1, self.near_sem))
            ]
            self.left = [
                remote(part(y, h), part(y, h), at_y(left), self.sent, at)
                for h, at in ((1, arrivals()), (0, self.near_sem))
            ]
            self.next_right = remote(part(left, 0), part(left, 0), at_y(right), self.sent, self.far_sem)
            self.next_left = remote(part(right, 1), part(right, 1), at_y(left), self.sent, self.far_sem)
            rings.append(self)

        def begin(self):
            for h in range(2):
                self.right[h].start()
                self.left[h].start()

        def relay(self):
            self.right[0].wait_recv()
            self.next_right.start()
            self.left[0].wait_recv()
            self.next_left.start()

        def near(self):
            wait(self.span(1), self.near_sem)

        def far(self):
            wait(self.span(1), self.far_sem)

        def finish(self):
            self.near()
            self.far()

        def end(self):
            wait(self.span(3), self.sent)

    class Rows:
        def __init__(self, part, whole, full, src, own, sem):
            self.whole, self.full = whole, full
            first = arrivals(3)
            goal = jnp.where(hub, pair, 3 - x)
            self.first_sent, self.next_sent, self.inside_sent = sends(), sends(), sends()
            self.pair_sem, self.next_sem, self.inside_sem = recv.at[first], arrivals(), arrivals()
            self.first = [
                remote(src(h), part(x, h), on(goal), self.first_sent, recv.at[first + jnp.where(hub, 0, 1 + h)])
                for h in (0, 1)
            ]
            self.far_in = [(part(3 - x, h), recv.at[first + 1 + h]) for h in (0, 1)]
            self.next = [
                remote(part(3 - x, h), part(3 - x, h), on(pair), self.next_sent, self.next_sem)
                for h in (0, 1)
            ]
            self.inside = [
                remote(whole(p), whole(p), other_core, self.inside_sent, self.inside_sem)
                for p in (x, 3 - x, pair, 3 - pair)
            ]
            self.local = pltpu.make_async_copy(own, whole(x), loc.at[sem])
            matrices.append(self)

        def begin(self):
            for h in range(2):
                self.first[h].start()

            @pl.when(hub)
            def _():
                self.local.start()

        def relay(self):
            @pl.when(hub)
            def _():
                self.local.wait()
                self.inside[0].start()
                for h in range(2):
                    wait(*self.far_in[h])
                    self.next[h].start()
                self.inside[1].start()

        def near(self):
            @pl.when(hub)
            def _():
                wait(self.whole(pair), self.pair_sem)
                self.inside[2].start()

        def pass_on(self):
            @pl.when(hub)
            def _():
                wait(self.whole(3 - pair), self.next_sem)
                self.inside[3].start()

        def finish(self):
            @pl.when(jnp.logical_not(hub))
            def _():
                wait(self.full, self.inside_sem)

        def end(self):
            wait(self.whole(0), self.first_sent)

            @pl.when(hub)
            def _():
                wait(self.whole(0), self.next_sent)
                wait(self.full, self.inside_sent)

    def halves(ref, size, *lead):
        return lambda p, h: ref.at[(*lead, pl.ds(p * size + h * (size // 2), size // 2), slice(None))]

    def wholes(ref, size, *lead):
        return lambda p: ref.at[(*lead, pl.ds(p * size, size), slice(None))]

    def span(ref, size, *lead):
        return lambda n: ref.at[(*lead, pl.ds(0, size * n), slice(None))]

    def of(ref, size, lane=slice(None)):
        return lambda h: ref.at[pl.ds(h * (size // 2), size // 2), lane]

    lanes_768 = [pl.ds(0, 768), pl.ds(768, 768)]

    barrier = pltpu.get_barrier_semaphore()
    peers = [at_y(lax.rem(y + d, 4)) for d in (1, 2, 3)]
    row_peers = [on(lax.rem(x + d, 4), core) for d in (1, 3, 2)]
    row_peers += [on(lax.rem(x + d, 4), 1 - core) for d in (0, 1, 3, 2)]
    for peer in peers + row_peers:
        pl.semaphore_signal(barrier, inc=1, device_id=peer, device_id_type=MESH)

    def lanes(t):
        return pl.ds(pl.multiple_of(t * 128, 128), 128)

    def tiles(p):
        return lanes(p + lax.div(p + 1, 2)), lanes(1 + 3 * lax.div(p, 2))

    full_tile, half_tile = tiles(col)
    moves = [
        (idx_in.at[pl.ds(pl.multiple_of(lax.div(leaf, 4) * 8, 8), 8), :], idx_s),
        (owner_in, owner),
        (e_in, e_raw.at[0]),
        (cf_in, c_raw.at[0]),
    ]
    moves = [pltpu.make_async_copy(src, dst, loc.at[i]) for i, (src, dst) in enumerate(moves)]
    own_idx, own_owner, own_e, own_cf = moves
    for copy in (own_owner, own_e, own_cf, own_idx):
        copy.start()

    e_cross = remote(e_in, e_raw.at[1], other_core, sends(), arrivals())
    c_cross = remote(cf_in, c_raw.at[1], other_core, sends(), arrivals())

    def e_rows(p):
        return e_s.at[:, pl.ds(y * 128 + p * 32, 32), :]

    e_at = arrivals(4)
    e_across, is_own = [], []
    for j in range(4):
        is_own.append(jnp.logical_and(hub, col == j))
        e_across.append(remote(
            e_sel.at[:, :, lanes(j)], e_rows(x), on(2 * core + j // 2, j % 2), sends(), recv.at[e_at + x]
        ))
    e_kept = pltpu.make_async_copy(e_sel.at[:, :, lanes(col)], e_rows(x), loc.at[4])

    rows_d = Rows(halves(d_s, 48), wholes(d_s, 48), d_s, of(d_in, 48), d_in, 5)
    rows_c = Rows(
        lambda p, h: cf_s.at[h, pl.ds(p * 64, 64), :], lambda p: cf_s.at[:, pl.ds(p * 64, 64), :], cf_s,
        lambda h: c_sel.at[h], c_sel, 6,
    )
    rows_f = Rows(halves(f_s, 96), wholes(f_s, 96), f_s, of(f_in, 96), f_in, 7)
    rows_b = [
        Rows(halves(b_s, 96, c), wholes(b_s, 96, c), b_s.at[c], of(b_in, 96, lanes_768[c]), b_in.at[:, lanes_768[c]], 8 + c)
        for c in range(2)
    ]
    ring_e = Ring(lambda p, h: e_s.at[h, pl.ds(p * 128, 128), :], lambda n: e_s.at[:, pl.ds(0, 128 * n), :])
    ring_dp = Ring(halves(v_s, 288), span(v_s, 288))
    ring_k = [Ring(halves(k_s, 256, c), span(k_s, 256, c)) for c in range(2)]
    ring_w = Ring(halves(w_s, 576), span(w_s, 576))
    ring_r = [Ring(halves(r_s, 384, c), span(r_s, 384, c)) for c in range(2)]
    w_pair = remote(w_x.at[col], w_x.at[col], on(pair), sends(), arrivals())
    w_in = remote(w_x.at[col], w_x.at[col], other_core, sends(), arrivals())
    far_col = 2 * lax.rem(pair, 2) + core
    w_on = remote(w_x.at[far_col], w_x.at[far_col], other_core, sends(), arrivals())

    pl.semaphore_wait(barrier, 10)

    e_cross.start()
    c_cross.start()
    rows_d.begin()

    def members(mine_leaf, other_leaf):
        pool = (2 * mine_leaf, 2 * mine_leaf + 1, 2 * other_leaf, 2 * other_leaf + 1)
        return pool, [(owner[p] == mine_leaf).astype(jnp.int32) for p in pool]

    def pick(c, flags, items):
        if c == 0:
            return select(flags[0], items[0], select(flags[1], items[1], items[2]))
        return select(flags[3], items[3], select(flags[2], items[2], items[1]))

    own_owner.wait()
    _, mine = members(leaf, partner)
    pool, held = members(base + group, base + 1 - group)
    own_e.wait()
    e_cross.wait_recv()
    for c in range(2):
        e_sel[c] = pick(c, mine, [e_raw[0, 0], e_raw[0, 1], e_raw[1, 0], e_raw[1, 1]])

    @pl.when(hub)
    def _():
        e_kept.start()

    for j in (2, 3, 0, 1):
        @pl.when(jnp.logical_not(is_own[j]))
        def _(j=j):
            e_across[j].start()

    rows_d.relay()
    own_cf.wait()
    c_cross.wait_recv()
    for c in range(2):
        for m in (0, 32):
            at = pl.ds(m, 32)
            c_sel[c, at, :] = pick(
                c, mine, [c_raw[0, 0, at, :], c_raw[0, 1, at, :], c_raw[1, 0, at, :], c_raw[1, 1, at, :]]
            )
    rows_c.begin()
    rows_d.near()

    own_idx.wait()
    idx_rows = [idx_s[pl.ds(lax.rem(p, 8), 1), :] for p in pool]

    def one_hot(c):
        positions = pick(c, held, idx_rows)
        for m in range(0, 768, 128):
            at = lax.broadcasted_iota(jnp.int32, (128, 1024), 0) + m
            su[c, pl.ds(m, 128), :] = jnp.where(at == positions, 1.0, 0.0).astype(BF16)
        for m in range(0, 384, 128):
            at = lax.broadcasted_iota(jnp.int32, (128, 1024), 0) + (768 + 384 * y + m)
            sl[c, pl.ds(m, 128), :] = jnp.where(at == positions, 1.0, 0.0).astype(BF16)

    def split_rows(src, hi, lo, size, step):
        for m in range(0, size, step):
            h, l = split(src[pl.ds(m, step), :])
            hi[pl.ds(m, step), :] = h
            lo[pl.ds(m, step), :] = l

    def split_to(value, hi, lo, row, lane):
        h, l = split(value)
        hi[row, pl.ds(lane, 128)] = h
        lo[row, pl.ds(lane, 128)] = l

    def low_lanes(shape):
        return lax.broadcasted_iota(jnp.int32, shape, 1) < 64

    def swap(value):
        return pltpu.roll(value, 64, 1)

    def pack(top, bottom):
        return jnp.where(low_lanes(top.shape), top, swap(bottom))

    @pl.when(hub)
    def _():
        e_kept.wait()

    for p in range(4):
        @pl.when(jnp.logical_not(jnp.logical_and(hub, x == p)))
        def _(p=p):
            wait(e_rows(p), recv.at[e_at + p])

    ring_e.begin()
    rows_d.pass_on()
    rows_c.relay()
    rows_f.begin()
    ring_e.relay()

    rows_d.finish()
    whole = d_s[:, full_tile]
    half = d_s[:, half_tile]
    half = select(core, swap(half), half)
    d_sums = [col_sum(whole * whole), col_sum(half * half)]
    v_s[pl.ds(pl.multiple_of(y * 288, 96), 192), :] = whole
    v_s[pl.ds(pl.multiple_of(y * 288 + 192, 96), 96), :] = pack(half[:96], half[96:])
    ring_dp.begin()
    one_hot(0)
    rows_c.near()

    ring_e.finish()
    e_sums = []
    for c in range(2):
        for m in range(0, 512, 128):
            h, l = split(e_s[c, pl.ds(m, 128), :])
            eh[c, pl.ds(m, 128), :] = h
            el[c, pl.ds(m, 128), :] = l
        part = e_s[c, pl.ds(pl.multiple_of(y * 128, 128), 128), :]
        e_sums.append(col_sum(part * part))
    rows_f.relay()
    rows_c.pass_on()
    rows_c.finish()
    ring_dp.relay()
    for c in range(2):
        for m in range(0, 256, 64):
            h, l = split(cf_s[c, pl.ds(m, 64), :])
            ch[c, pl.ds(m, 64), :] = h
            cl[c, pl.ds(m, 64), :] = l
        for m in range(0, 256, 128):
            at = pl.ds(m, 128)
            k_s[c, pl.ds(pl.multiple_of(y * 256 + m, 128), 128), :] = dot3(ch[c, at, :], cl[c, at, :], eh[c], el[c])
        ring_k[c].begin()
    rows_b[0].begin()
    rows_f.near()
    one_hot(1)
    split_rows(d_s, dh, dl, 192, 48)

    ring_dp.finish()
    for p in range(4):
        for m in (0, 96):
            split_to(v_s[pl.ds(288 * p + m, 96), :], vh, vl, pl.ds(192 * p + m, 96), 0)
            value = v_s[pl.ds(288 * p + 192, 96), :]
            split_to(swap(value) if m else value, vh, vl, pl.ds(192 * p + m, 96), 128)
    ring_k[0].relay()
    rows_f.pass_on()
    rows_f.finish()
    split_rows(f_s, fh, fl, 384, 48)
    for m in (0, 192):
        at = pl.ds(m, 192)
        value = dot3(fh[at, :], fl[at, :], vh[...], vl[...])
        w_s[pl.ds(pl.multiple_of(y * 576 + m, 192), 192), :] = value[:, :128]
        w_x[col, at, :] = value[:, :128]
        w_half[at, :] = value[:, 128:]
    packed = pack(w_half[0:192, :], w_half[192:384, :])
    w_s[pl.ds(pl.multiple_of(y * 576 + 384, 192), 192), :] = packed
    w_x[col, pl.ds(384, 192), :] = packed
    w_pair.start()
    w_in.start()
    ring_k[1].relay()
    ring_w.begin()
    rows_b[0].relay()
    rows_b[1].begin()

    for c in range(2):
        ring_k[c].finish()
        for m in range(0, 1024, 128):
            h, l = split(k_s[c, pl.ds(m, 128), :])
            kh[c, pl.ds(m, 128), :] = h
            kl[c, pl.ds(m, 128), :] = l
        for m in range(0, 768, 256):
            at = pl.ds(m, 256)
            uh[at, pl.ds(c * 128, 128)] = dot(su[c, at, :], kh[c]).astype(BF16)
            ul[at, pl.ds(c * 128, 128)] = dot(su[c, at, :], kl[c]).astype(BF16)
        if c == 0:
            ring_w.relay()
        else:
            w_pair.wait_recv()
            w_on.start()
        for m in range(0, 384, 128):
            at = pl.ds(m, 128)
            l_s[at, pl.ds(c * 128, 128)] = dot(sl[c, at, :], kh[c]) + dot(sl[c, at, :], kl[c])

    rows_b[0].near()
    rows_b[1].relay()
    w_in.wait_recv()
    w_on.wait_recv()
    for p, t in enumerate((0, 2, 3, 5)):
        for m in (0, 192):
            split_to(w_x[p, pl.ds(m, 192), :], wh, wl, pl.ds(m, 192), 128 * t)
    for p, t in ((0, 1), (2, 4)):
        low, high = w_x[p, pl.ds(384, 192), :], w_x[p + 1, pl.ds(384, 192), :]
        split_to(jnp.where(low_lanes(low.shape), low, swap(high)), wh, wl, pl.ds(0, 192), 128 * t)
        split_to(jnp.where(low_lanes(low.shape), swap(low), high), wh, wl, pl.ds(192, 192), 128 * t)
    for c in range(2):
        cols = pl.ds(c * 128, 128)
        for m in (0, 192):
            at = pl.ds(m, 192)
            value = l_s[at, cols] - dot3(wh[at, :], wl[at, :], uh[:, cols], ul[:, cols])
            r_s[c, pl.ds(pl.multiple_of(y * 384 + m, 192), 192), :] = value
        ring_r[c].begin()
    rows_b[0].pass_on()
    rows_b[1].near()
    value = dot3(dh[...], dl[...], uh[...], ul[...])
    v_sums = col_sum(value * value)
    ring_r[0].relay()
    rows_b[1].pass_on()
    ring_r[1].relay()
    ring_w.finish()
    for c in range(2):
        rows_b[c].finish()
        split_rows(b_s.at[c], bh.at[:, lanes_768[c]], bl.at[:, lanes_768[c]], 384, 48)

    for p in range(4):
        for m in (0, 192):
            row = pl.ds(p * 384 + m, 192)
            split_to(w_s[pl.ds(p * 576 + m, 192), :], rh, rl, row, 0)
            value = w_s[pl.ds(p * 576 + 384, 192), :]
            split_to(swap(value) if m else value, rh, rl, row, 128)
    p_sums = [jnp.zeros((1, 128), F32)] * 2
    for m in range(0, 384, 128):
        at = pl.ds(m, 128)
        value = dot3(bh[at, :], bl[at, :], rh[...], rl[...])
        to = pl.ds(pl.multiple_of(y * 576 + m, 64), 128)
        p_sums[0] = p_sums[0] + col_sum(value[:, :128] * w_s[to, :])
        p_sums[1] = p_sums[1] + col_sum(value[:, 128:] * w_half[at, :])

    def add_rows(p, first):
        row = pl.ds(pl.multiple_of(p * 384, 384), 384)
        for c in range(2):
            split_to(r_s[c, row, :], rh, rl, row, 128 * c)
        cols = pl.ds(pl.multiple_of(p * 384, 128), 384)
        for m in range(0, 384, 128):
            at = pl.ds(m, 128)
            value = dot3(bh[at, cols], bl[at, cols], rh[row, :], rl[row, :])
            acc[at, :] = value if first else acc[at, :] + value

    add_rows(y, True)
    for c in range(2):
        ring_r[c].near()
    add_rows(lax.rem(y + 1, 4), False)
    add_rows(lax.rem(y + 3, 4), False)
    for c in range(2):
        ring_r[c].far()
    add_rows(lax.rem(y + 2, 4), False)
    c_sums = [v_sums[:, c * 128:(c + 1) * 128] for c in range(2)]
    for m in range(0, 384, 128):
        to = pl.ds(pl.multiple_of(y * 384 + m, 128), 128)
        for c in range(2):
            c_sums[c] = c_sums[c] + col_sum(acc[pl.ds(m, 128), c * 128:(c + 1) * 128] * r_s[c, to, :])

    for c in range(2):
        stage[c:c + 1, :] = p_sums[c]
        stage[2 + c:3 + c, :] = c_sums[c]
        stage[4 + c:5 + c, :] = d_sums[c]
        stage[6 + c:7 + c, :] = e_sums[c]
    fin[y] = stage[...]
    sent, arrived = sends(), arrivals()
    for d in (1, 3, 2):
        remote(stage, fin.at[y], at_y(lax.rem(y + d, 4)), sent, arrived).start()
    wait(fin.at[pl.ds(0, 3)], arrived)
    ostage[...] = ((fin[0] + fin[1]) + fin[2]) + fin[3]
    place = 4 * group + col
    xfin[place] = ostage[...]
    last_sent, arrived = sends(), arrivals()
    for peer in row_peers:
        remote(ostage, xfin.at[place], peer, last_sent, arrived).start()
    wait(xfin.at[pl.ds(0, 7)], arrived)
    before = 2 - mine[2] - mine[3]
    for j, t in enumerate((0, 2, 3, 5)):
        own, other = xfin[4 * core + j], xfin[4 - 4 * core + j]
        for ref, r in ((out_c, 2), (out_e, 6)):
            first = select(before, other[r + 1:r + 2], other[r:r + 1])
            ref[0:1, j * 128:(j + 1) * 128] = select(mine[0], own[r:r + 1], first)
            second = select(mine[0], own[r + 1:r + 2], own[r:r + 1])
            ref[1:2, j * 128:(j + 1) * 128] = select(mine[1], second, other[r + 1:r + 2])
        for ref, r in ((out_p, 0), (out_d, 4)):
            ref[:, t * 128:(t + 1) * 128] = own[r:r + 1]
            if j in (0, 2):
                after = xfin[4 * core + j + 1]
                ref[:, (t + 1) * 128:(t + 2) * 128] = pack(own[r + 1:r + 2], after[r + 1:r + 2])
    for each in rings + matrices:
        each.end()
    for copy in [e_cross, c_cross, w_pair, w_in, w_on]:
        copy.wait_send()
    for j in range(4):
        @pl.when(jnp.logical_not(is_own[j]))
        def _(j=j):
            e_across[j].wait_send()

    wait(fin.at[pl.ds(0, 3)], sent)
    wait(xfin.at[pl.ds(0, 7)], last_sent)
    assert taken == [SENDS, ARRIVALS], taken


SENDS, ARRIVALS = 33, 64


def shards(b, f, d, cf, e, idx, owner):
    vm = pltpu.VMEM
    any_spec = pl.BlockSpec(memory_space=pl.ANY)
    vmem_spec = pl.BlockSpec(memory_space=pltpu.VMEM)
    row, kid = jax.ShapeDtypeStruct((1, 768), F32), jax.ShapeDtypeStruct((2, 512), F32)
    quad_p, diag_p, quad_c, diag_c = pl.pallas_call(
        kernel,
        out_shape=(row, row, kid, kid),
        in_specs=[any_spec] * 7,
        out_specs=(vmem_spec,) * 4,
        scratch_shapes=[
            vm((2, 2, 32, 512), F32), vm((2, 2, 64, 512), F32), vm((2, 32, 512), F32), vm((2, 64, 512), F32),
            vm((2, 384, 768), F32), vm((384, 768), F32), vm((192, 768), F32),
            vm((2, 256, 512), F32), vm((2, 512, 128), F32),
            vm((2, 1024, 128), F32), vm((1152, 128), F32),
            vm((2, 1536, 128), F32), vm((384, 128), F32), vm((2304, 128), F32), vm((4, 576, 128), F32),
            vm((8, 1024), jnp.int32), vm((384, 256), F32), vm((384, 256), F32),
            pltpu.SMEM((64,), jnp.int32),
            vm((2, 768, 1024), BF16), vm((2, 384, 1024), BF16),
            vm((384, 1536), BF16), vm((384, 1536), BF16),
            vm((384, 768), BF16), vm((384, 768), BF16),
            vm((192, 768), BF16), vm((192, 768), BF16),
            vm((2, 256, 512), BF16), vm((2, 256, 512), BF16),
            vm((2, 512, 128), BF16), vm((2, 512, 128), BF16),
            vm((2, 1024, 128), BF16), vm((2, 1024, 128), BF16),
            vm((768, 256), BF16), vm((768, 256), BF16),
            vm((768, 256), BF16), vm((768, 256), BF16),
            vm((384, 768), BF16), vm((384, 768), BF16),
            vm((1536, 256), BF16), vm((1536, 256), BF16),
            vm((8, 128), F32), vm((4, 8, 128), F32), vm((8, 128), F32), vm((8, 8, 128), F32),
            pltpu.SemaphoreType.DMA((SENDS,)),
            pltpu.SemaphoreType.DMA((ARRIVALS,)),
            pltpu.SemaphoreType.DMA((10,)),
        ],
        compiler_params=pltpu.CompilerParams(
            collective_id=0, has_side_effects=True, vmem_limit_bytes=60 * 1024 * 1024
        ),
        name="selected",
    )(b[0], f[0], d[0], cf, e, idx, owner)
    return diag_p + quad_p, diag_c + quad_c


def solution(mesh):
    split_spec = P("leaf", "front", None)
    in_specs = (split_spec,) * 5 + (P(), P())
    out_specs = (P("leaf", None), P("leaf", None))
    return jax.shard_map(shards, mesh=mesh, in_specs=in_specs, out_specs=out_specs, check_vma=False)
```

```python
import jax
import jax.numpy as jnp
from jax import lax
from jax.experimental import pallas as pl
from jax.experimental.pallas import tpu as pltpu
from jax.sharding import PartitionSpec as P

F32 = jnp.float32
BF16 = jnp.bfloat16
MESH = pl.DeviceIdType.MESH


def dot(a, b):
    return jnp.dot(a, b, preferred_element_type=F32)


def dot3(ah, al, bh, bl):
    return dot(ah, bh) + (dot(ah, bl) + dot(al, bh))


def split(x):
    hi = x.astype(BF16)
    return hi, (x - hi.astype(F32)).astype(BF16)


def col_sum(x):
    return jnp.sum(x, axis=0, keepdims=True)


def select(flag, yes, no):
    return jnp.where(jnp.full(yes.shape, flag, jnp.int32) == 1, yes, no)


def kernel(
    b_in, f_in, d_in, cf_in, e_in, idx_in, owner_in,
    out_p, out_d, out_c, out_e,
    e_raw, c_raw, e_sel, c_sel,
    b_s, f_s, d_s, cf_s, e_s, k_s, v_s, u_s, w_half, w_s, w_x,
    idx_s, r_own, acc, owner,
    place, bh, bl, fh, fl, dh, dl, ch, cl, eh, el, kk, uh, ul, vh, vl, wh, wl, rh, rl, lh, ll,
    stage, fin, ostage, xfin, send, recv, loc,
):
    leaf = lax.axis_index("leaf")
    front = lax.axis_index("front")
    y = lax.div(front, 4)
    x = lax.rem(front, 4)
    core = lax.rem(leaf, 2)
    base = leaf - core
    partner = base + 1 - core
    group = lax.div(x, 2)
    pair = x + 1 - 2 * lax.rem(x, 2)
    col = 2 * lax.rem(x, 2) + core
    hub = core == group
    taken = [0, 0]

    def sends():
        taken[0] += 1
        return send.at[taken[0] - 1]

    def arrivals(n=1):
        taken[1] += n
        return recv.at[taken[1] - 1] if n == 1 else taken[1] - n

    def remote(src, dst, device, sent, arrived):
        return pltpu.make_async_remote_copy(
            src_ref=src, dst_ref=dst, send_sem=sent, recv_sem=arrived,
            device_id=device, device_id_type=MESH,
        )

    def wait(ref, sem):
        pltpu.make_async_copy(ref, ref, sem).wait()

    def at_y(p):
        return {"front": p * 4 + x}

    def on(chip, a_core=None):
        if a_core is None:
            return {"front": y * 4 + chip}
        return {"leaf": base + a_core, "front": y * 4 + chip}

    other_core = {"leaf": partner}

    rings, matrices = [], []

    class Ring:
        def __init__(self, part, span):
            right, left = lax.rem(y + 1, 4), lax.rem(y + 3, 4)
            self.span, self.sent = span, sends()
            self.near_sem, self.far_sem = arrivals(), arrivals()
            self.right = [
                remote(part(y, h), part(y, h), at_y(right), self.sent, at)
                for h, at in ((0, arrivals()), (1, self.near_sem))
            ]
            self.left = [
                remote(part(y, h), part(y, h), at_y(left), self.sent, at)
                for h, at in ((1, arrivals()), (0, self.near_sem))
            ]
            self.next_right = remote(part(left, 0), part(left, 0), at_y(right), self.sent, self.far_sem)
            self.next_left = remote(part(right, 1), part(right, 1), at_y(left), self.sent, self.far_sem)
            rings.append(self)

        def begin(self):
            for h in range(2):
                self.right[h].start()
                self.left[h].start()

        def relay(self):
            self.right[0].wait_recv()
            self.next_right.start()
            self.left[0].wait_recv()
            self.next_left.start()

        def near(self):
            wait(self.span(1), self.near_sem)

        def far(self):
            wait(self.span(1), self.far_sem)

        def finish(self):
            self.near()
            self.far()

        def end(self):
            wait(self.span(3), self.sent)

    class Rows:
        def __init__(self, part, whole, full, src, own, sem):
            self.whole, self.full = whole, full
            first = arrivals(3)
            goal = jnp.where(hub, pair, 3 - x)
            self.first_sent, self.next_sent, self.inside_sent = sends(), sends(), sends()
            self.pair_sem, self.next_sem, self.inside_sem = recv.at[first], arrivals(), arrivals()
            self.first = [
                remote(src(h), part(x, h), on(goal), self.first_sent, recv.at[first + jnp.where(hub, 0, 1 + h)])
                for h in (0, 1)
            ]
            self.far_in = [(part(3 - x, h), recv.at[first + 1 + h]) for h in (0, 1)]
            self.next = [
                remote(part(3 - x, h), part(3 - x, h), on(pair), self.next_sent, self.next_sem)
                for h in (0, 1)
            ]
            self.inside = [
                remote(whole(p), whole(p), other_core, self.inside_sent, self.inside_sem)
                for p in (x, 3 - x, pair, 3 - pair)
            ]
            self.local = pltpu.make_async_copy(own, whole(x), loc.at[sem])
            matrices.append(self)

        def begin(self):
            for h in range(2):
                self.first[h].start()

            @pl.when(hub)
            def _():
                self.local.start()

        def relay(self):
            @pl.when(hub)
            def _():
                self.local.wait()
                self.inside[0].start()
                for h in range(2):
                    wait(*self.far_in[h])
                    self.next[h].start()
                self.inside[1].start()

        def near(self):
            @pl.when(hub)
            def _():
                wait(self.whole(pair), self.pair_sem)
                self.inside[2].start()

        def pass_on(self):
            @pl.when(hub)
            def _():
                wait(self.whole(3 - pair), self.next_sem)
                self.inside[3].start()

        def finish(self):
            @pl.when(jnp.logical_not(hub))
            def _():
                wait(self.full, self.inside_sem)

        def end(self):
            wait(self.whole(0), self.first_sent)

            @pl.when(hub)
            def _():
                wait(self.whole(0), self.next_sent)
                wait(self.full, self.inside_sent)

    def halves(ref, size, *lead):
        return lambda p, h: ref.at[(*lead, pl.ds(p * size + h * (size // 2), size // 2), slice(None))]

    def wholes(ref, size, *lead):
        return lambda p: ref.at[(*lead, pl.ds(p * size, size), slice(None))]

    def span(ref, size, *lead):
        return lambda n: ref.at[(*lead, pl.ds(0, size * n), slice(None))]

    def of(ref, size, lane=slice(None)):
        return lambda h: ref.at[pl.ds(h * (size // 2), size // 2), lane]

    lanes_768 = [pl.ds(0, 768), pl.ds(768, 768)]

    barrier = pltpu.get_barrier_semaphore()
    peers = [at_y(lax.rem(y + d, 4)) for d in (1, 2, 3)]
    row_peers = [on(lax.rem(x + d, 4), core) for d in (1, 3, 2)]
    row_peers += [on(lax.rem(x + d, 4), 1 - core) for d in (0, 1, 3, 2)]
    for peer in peers + row_peers:
        pl.semaphore_signal(barrier, inc=1, device_id=peer, device_id_type=MESH)

    def lanes(t):
        return pl.ds(pl.multiple_of(t * 128, 128), 128)

    def tiles(p):
        return lanes(p + lax.div(p + 1, 2)), lanes(1 + 3 * lax.div(p, 2))

    full_tile, half_tile = tiles(col)
    moves = [
        (idx_in.at[pl.ds(pl.multiple_of(lax.div(leaf, 4) * 8, 8), 8), :], idx_s),
        (owner_in, owner),
        (e_in, e_raw.at[0]),
        (cf_in, c_raw.at[0]),
    ]
    moves = [pltpu.make_async_copy(src, dst, loc.at[i]) for i, (src, dst) in enumerate(moves)]
    own_idx, own_owner, own_e, own_cf = moves
    for copy in (own_owner, own_e, own_cf, own_idx):
        copy.start()

    e_cross = remote(e_in, e_raw.at[1], other_core, sends(), arrivals())
    c_cross = remote(cf_in, c_raw.at[1], other_core, sends(), arrivals())

    def e_rows(p):
        return e_s.at[:, pl.ds(y * 128 + p * 32, 32), :]

    e_at = arrivals(4)
    e_across, is_own = [], []
    for j in range(4):
        is_own.append(jnp.logical_and(hub, col == j))
        e_across.append(remote(
            e_sel.at[:, :, lanes(j)], e_rows(x), on(2 * core + j // 2, j % 2), sends(), recv.at[e_at + x]
        ))
    e_kept = pltpu.make_async_copy(e_sel.at[:, :, lanes(col)], e_rows(x), loc.at[4])

    rows_d = Rows(halves(d_s, 48), wholes(d_s, 48), d_s, of(d_in, 48), d_in, 5)
    rows_c = Rows(
        lambda p, h: cf_s.at[h, pl.ds(p * 64, 64), :], lambda p: cf_s.at[:, pl.ds(p * 64, 64), :], cf_s,
        lambda h: c_sel.at[h], c_sel, 6,
    )
    rows_f = Rows(halves(f_s, 96), wholes(f_s, 96), f_s, of(f_in, 96), f_in, 7)
    rows_b = [
        Rows(halves(b_s, 96, c), wholes(b_s, 96, c), b_s.at[c], of(b_in, 96, lanes_768[c]), b_in.at[:, lanes_768[c]], 8 + c)
        for c in range(2)
    ]
    ring_e = Ring(lambda p, h: e_s.at[h, pl.ds(p * 128, 128), :], lambda n: e_s.at[:, pl.ds(0, 128 * n), :])
    ring_dp = Ring(halves(v_s, 288), span(v_s, 288))
    ring_k = [Ring(halves(k_s, 256, c), span(k_s, 256, c)) for c in range(2)]
    ring_w = Ring(halves(w_s, 576), span(w_s, 576))
    ring_v = Ring(
        lambda p, h: u_s.at[h, pl.ds(p * 192, 192), :], lambda n: u_s.at[:, pl.ds(0, 192 * n), :]
    )
    far_col = 2 * lax.rem(pair, 2) + core
    w_pair, w_in, w_on = [], [], []
    for rows in (pl.ds(0, 384), pl.ds(384, 192)):
        near, far = w_x.at[col, rows, :], w_x.at[far_col, rows, :]
        w_pair.append(remote(near, near, on(pair), sends(), arrivals()))
        w_in.append(remote(near, near, other_core, sends(), arrivals()))
        w_on.append(remote(far, far, other_core, sends(), arrivals()))

    pl.semaphore_wait(barrier, 10)

    e_cross.start()
    c_cross.start()
    rows_d.begin()

    def members(mine_leaf, other_leaf):
        pool = (2 * mine_leaf, 2 * mine_leaf + 1, 2 * other_leaf, 2 * other_leaf + 1)
        return pool, [(owner[p] == mine_leaf).astype(jnp.int32) for p in pool]

    def pick(c, flags, items):
        if c == 0:
            return select(flags[0], items[0], select(flags[1], items[1], items[2]))
        return select(flags[3], items[3], select(flags[2], items[2], items[1]))

    own_owner.wait()
    _, mine = members(leaf, partner)
    pool, held = members(base + group, base + 1 - group)
    own_e.wait()
    e_cross.wait_recv()
    for c in range(2):
        e_sel[c] = pick(c, mine, [e_raw[0, 0], e_raw[0, 1], e_raw[1, 0], e_raw[1, 1]])

    @pl.when(hub)
    def _():
        e_kept.start()

    for j in (2, 3, 0, 1):
        @pl.when(jnp.logical_not(is_own[j]))
        def _(j=j):
            e_across[j].start()

    rows_d.relay()
    own_cf.wait()
    c_cross.wait_recv()
    for c in range(2):
        for m in (0, 32):
            at = pl.ds(m, 32)
            c_sel[c, at, :] = pick(
                c, mine, [c_raw[0, 0, at, :], c_raw[0, 1, at, :], c_raw[1, 0, at, :], c_raw[1, 1, at, :]]
            )
    rows_c.begin()
    rows_d.near()

    own_idx.wait()
    idx_rows = [idx_s[pl.ds(lax.rem(p, 8), 1), :] for p in pool]

    def one_hot(c):
        positions = pick(c, held, idx_rows)
        for m in range(0, 2304, 128):
            at = lax.broadcasted_iota(jnp.int32, (128, 1024), 0) + m
            place[c, pl.ds(m, 128), :] = jnp.where(at == positions, 1.0, 0.0).astype(BF16)

    def split_rows(src, hi, lo, size, step):
        for m in range(0, size, step):
            h, l = split(src[pl.ds(m, step), :])
            hi[pl.ds(m, step), :] = h
            lo[pl.ds(m, step), :] = l

    def split_to(value, hi, lo, row, lane):
        h, l = split(value)
        hi[row, pl.ds(lane, 128)] = h
        lo[row, pl.ds(lane, 128)] = l

    def low_lanes(shape):
        return lax.broadcasted_iota(jnp.int32, shape, 1) < 64

    def swap(value):
        return pltpu.roll(value, 64, 1)

    def pack(top, bottom):
        return jnp.where(low_lanes(top.shape), top, swap(bottom))

    @pl.when(hub)
    def _():
        e_kept.wait()

    for p in range(4):
        @pl.when(jnp.logical_not(jnp.logical_and(hub, x == p)))
        def _(p=p):
            wait(e_rows(p), recv.at[e_at + p])

    ring_e.begin()
    rows_d.pass_on()
    rows_c.relay()
    rows_f.begin()
    ring_e.relay()

    rows_d.finish()
    whole = d_s[:, full_tile]
    half = d_s[:, half_tile]
    half = select(core, swap(half), half)
    d_sums = [col_sum(whole * whole), col_sum(half * half)]
    v_s[pl.ds(pl.multiple_of(y * 288, 96), 192), :] = whole
    v_s[pl.ds(pl.multiple_of(y * 288 + 192, 96), 96), :] = pack(half[:96], half[96:])
    ring_dp.begin()
    one_hot(0)
    rows_c.near()

    ring_e.finish()
    e_sums = []
    for c in range(2):
        for m in range(0, 512, 128):
            h, l = split(e_s[c, pl.ds(m, 128), :])
            eh[c, pl.ds(m, 128), :] = h
            el[c, pl.ds(m, 128), :] = l
        part = e_s[c, pl.ds(pl.multiple_of(y * 128, 128), 128), :]
        e_sums.append(col_sum(part * part))
    rows_f.relay()
    rows_c.pass_on()
    rows_c.finish()
    ring_dp.relay()
    for c in range(2):
        for m in range(0, 256, 64):
            h, l = split(cf_s[c, pl.ds(m, 64), :])
            ch[c, pl.ds(m, 64), :] = h
            cl[c, pl.ds(m, 64), :] = l
        for m in range(0, 256, 128):
            at = pl.ds(m, 128)
            k_s[c, pl.ds(pl.multiple_of(y * 256 + m, 128), 128), :] = dot3(ch[c, at, :], cl[c, at, :], eh[c], el[c])
        ring_k[c].begin()
    rows_b[0].begin()
    rows_f.near()
    one_hot(1)
    split_rows(d_s, dh, dl, 192, 48)

    ring_dp.finish()
    for p in range(4):
        for m in (0, 96):
            split_to(v_s[pl.ds(288 * p + m, 96), :], vh, vl, pl.ds(192 * p + m, 96), 0)
            value = v_s[pl.ds(288 * p + 192, 96), :]
            split_to(swap(value) if m else value, vh, vl, pl.ds(192 * p + m, 96), 128)
    ring_k[0].relay()
    rows_f.pass_on()
    rows_f.finish()
    split_rows(f_s, fh, fl, 384, 48)
    for m in (0, 192):
        at = pl.ds(m, 192)
        value = dot3(fh[at, :], fl[at, :], vh[...], vl[...])
        w_s[pl.ds(pl.multiple_of(y * 576 + m, 192), 192), :] = value[:, :128]
        w_half[at, :] = value[:, 128:]
    packed = pack(w_half[0:192, :], w_half[192:384, :])
    w_s[pl.ds(pl.multiple_of(y * 576 + 384, 192), 192), :] = packed
    ring_k[1].relay()
    ring_w.begin()
    rows_b[0].relay()
    rows_b[1].begin()

    v_sums = []
    for c in range(2):
        ring_k[c].finish()
        for m in range(0, 1024, 128):
            h, l = split(k_s[c, pl.ds(m, 128), :])
            kk[c, pl.ds(m, 128), pl.ds(0, 128)] = h
            kk[c, pl.ds(m, 128), pl.ds(128, 128)] = l
        cols = pl.ds(c * 128, 128)
        for m in range(0, 768, 256):
            at = pl.ds(m, 256)
            value = dot(place[c, at, :], kk[c]).astype(BF16)
            uh[at, cols] = value[:, :128]
            ul[at, cols] = value[:, 128:]
        if c == 0:
            ring_w.relay()
            rows_b[0].near()
            rows_b[1].relay()
        value = dot3(dh[...], dl[...], uh[:, cols], ul[:, cols])
        u_s[c, pl.ds(pl.multiple_of(y * 192, 192), 192), :] = value
        v_sums.append(col_sum(value * value))
    ring_v.begin()
    rows_b[0].pass_on()
    rows_b[1].near()
    for c in range(2):
        cols = pl.ds(c * 128, 128)
        for m in range(0, 1536, 256):
            at = pl.ds(m, 256)
            value = dot(place[c, pl.ds(768 + m, 256), :], kk[c]).astype(BF16)
            lh[at, cols] = value[:, :128]
            ll[at, cols] = value[:, 128:]
    rows_b[1].pass_on()
    ring_w.finish()
    for c in range(2):
        rows_b[c].finish()
        split_rows(b_s.at[c], bh.at[:, lanes_768[c]], bl.at[:, lanes_768[c]], 384, 48)

    for p in range(4):
        for m in (0, 192):
            row = pl.ds(p * 384 + m, 192)
            split_to(w_s[pl.ds(p * 576 + m, 192), :], rh, rl, row, 0)
            value = w_s[pl.ds(p * 576 + 384, 192), :]
            split_to(swap(value) if m else value, rh, rl, row, 128)
    p_sums = [jnp.zeros((1, 128), F32)] * 2
    for m in range(0, 384, 128):
        at = pl.ds(m, 128)
        value = dot3(bh[at, :], bl[at, :], rh[...], rl[...])
        to = pl.ds(pl.multiple_of(y * 576 + m, 64), 128)
        p_sums[0] = p_sums[0] + col_sum(value[:, :128] * w_s[to, :])
        p_sums[1] = p_sums[1] + col_sum(value[:, 128:] * w_half[at, :])
        w_x[col, at, :] = value[:, :128]
        w_half[at, :] = value[:, 128:]
    w_x[col, pl.ds(384, 192), :] = pack(w_half[0:192, :], w_half[192:384, :])
    for n in range(2):
        w_pair[n].start()
        w_in[n].start()
    ring_v.relay()

    for m in range(0, 384, 128):
        at = pl.ds(m, 128)
        acc[at, :] = dot3(bh[at, :], bl[at, :], lh[...], ll[...])
    ring_v.finish()
    for c in range(2):
        for m in range(0, 768, 128):
            split_to(u_s[c, pl.ds(m, 128), :], vh, vl, pl.ds(m, 128), 128 * c)
    for m in range(0, 384, 128):
        at = pl.ds(m, 128)
        to = pl.ds(pl.multiple_of(y * 384 + m, 128), 128)
        value = lh[to, :].astype(F32) + ll[to, :].astype(F32)
        r_own[at, :] = value - dot3(fh[at, :], fl[at, :], vh[...], vl[...])
    for n in range(2):
        w_pair[n].wait_recv()
        w_on[n].start()
    for n in range(2):
        w_in[n].wait_recv()
        w_on[n].wait_recv()
    for p, t in enumerate((0, 2, 3, 5)):
        for m in (0, 192):
            split_to(w_x[p, pl.ds(m, 192), :], wh, wl, pl.ds(m, 192), 128 * t)
    for p, t in ((0, 1), (2, 4)):
        low, high = w_x[p, pl.ds(384, 192), :], w_x[p + 1, pl.ds(384, 192), :]
        split_to(jnp.where(low_lanes(low.shape), low, swap(high)), wh, wl, pl.ds(0, 192), 128 * t)
        split_to(jnp.where(low_lanes(low.shape), swap(low), high), wh, wl, pl.ds(192, 192), 128 * t)
    c_sums = v_sums
    for m in range(0, 384, 128):
        at = pl.ds(m, 128)
        value = acc[at, :] - dot3(wh[at, :], wl[at, :], uh[...], ul[...])
        value = col_sum(value * r_own[at, :])
        c_sums = [c_sums[c] + value[:, c * 128:(c + 1) * 128] for c in range(2)]

    for c in range(2):
        stage[c:c + 1, :] = p_sums[c]
        stage[2 + c:3 + c, :] = c_sums[c]
        stage[4 + c:5 + c, :] = d_sums[c]
        stage[6 + c:7 + c, :] = e_sums[c]
    fin[y] = stage[...]
    sent, arrived = sends(), arrivals()
    for d in (1, 3, 2):
        remote(stage, fin.at[y], at_y(lax.rem(y + d, 4)), sent, arrived).start()
    wait(fin.at[pl.ds(0, 3)], arrived)
    ostage[...] = ((fin[0] + fin[1]) + fin[2]) + fin[3]
    my_place = 4 * group + col
    xfin[my_place] = ostage[...]
    last_sent, arrived = sends(), arrivals()
    for peer in row_peers:
        remote(ostage, xfin.at[my_place], peer, last_sent, arrived).start()
    wait(xfin.at[pl.ds(0, 7)], arrived)
    before = 2 - mine[2] - mine[3]
    for j, t in enumerate((0, 2, 3, 5)):
        own, other = xfin[4 * core + j], xfin[4 - 4 * core + j]
        for ref, r in ((out_c, 2), (out_e, 6)):
            first = select(before, other[r + 1:r + 2], other[r:r + 1])
            ref[0:1, j * 128:(j + 1) * 128] = select(mine[0], own[r:r + 1], first)
            second = select(mine[0], own[r + 1:r + 2], own[r:r + 1])
            ref[1:2, j * 128:(j + 1) * 128] = select(mine[1], second, other[r + 1:r + 2])
        for ref, r in ((out_p, 0), (out_d, 4)):
            ref[:, t * 128:(t + 1) * 128] = own[r:r + 1]
            if j in (0, 2):
                after = xfin[4 * core + j + 1]
                ref[:, (t + 1) * 128:(t + 2) * 128] = pack(own[r + 1:r + 2], after[r + 1:r + 2])
    for each in rings + matrices:
        each.end()
    for copy in [e_cross, c_cross] + w_pair + w_in + w_on:
        copy.wait_send()
    for j in range(4):
        @pl.when(jnp.logical_not(is_own[j]))
        def _(j=j):
            e_across[j].wait_send()

    wait(fin.at[pl.ds(0, 3)], sent)
    wait(xfin.at[pl.ds(0, 7)], last_sent)
    assert taken == [SENDS, ARRIVALS], taken


SENDS, ARRIVALS = 35, 63


def shards(b, f, d, cf, e, idx, owner):
    vm = pltpu.VMEM
    any_spec = pl.BlockSpec(memory_space=pl.ANY)
    vmem_spec = pl.BlockSpec(memory_space=pltpu.VMEM)
    row, kid = jax.ShapeDtypeStruct((1, 768), F32), jax.ShapeDtypeStruct((2, 512), F32)
    quad_p, diag_p, quad_c, diag_c = pl.pallas_call(
        kernel,
        out_shape=(row, row, kid, kid),
        in_specs=[any_spec] * 7,
        out_specs=(vmem_spec,) * 4,
        scratch_shapes=[
            vm((2, 2, 32, 512), F32), vm((2, 2, 64, 512), F32), vm((2, 32, 512), F32), vm((2, 64, 512), F32),
            vm((2, 384, 768), F32), vm((384, 768), F32), vm((192, 768), F32),
            vm((2, 256, 512), F32), vm((2, 512, 128), F32),
            vm((2, 1024, 128), F32), vm((1152, 128), F32),
            vm((2, 768, 128), F32), vm((384, 128), F32), vm((2304, 128), F32), vm((4, 576, 128), F32),
            vm((8, 1024), jnp.int32), vm((384, 256), F32), vm((384, 256), F32),
            pltpu.SMEM((64,), jnp.int32),
            vm((2, 2304, 1024), BF16),
            vm((384, 1536), BF16), vm((384, 1536), BF16),
            vm((384, 768), BF16), vm((384, 768), BF16),
            vm((192, 768), BF16), vm((192, 768), BF16),
            vm((2, 256, 512), BF16), vm((2, 256, 512), BF16),
            vm((2, 512, 128), BF16), vm((2, 512, 128), BF16),
            vm((2, 1024, 256), BF16),
            vm((768, 256), BF16), vm((768, 256), BF16),
            vm((768, 256), BF16), vm((768, 256), BF16),
            vm((384, 768), BF16), vm((384, 768), BF16),
            vm((1536, 256), BF16), vm((1536, 256), BF16),
            vm((1536, 256), BF16), vm((1536, 256), BF16),
            vm((8, 128), F32), vm((4, 8, 128), F32), vm((8, 128), F32), vm((8, 8, 128), F32),
            pltpu.SemaphoreType.DMA((SENDS,)),
            pltpu.SemaphoreType.DMA((ARRIVALS,)),
            pltpu.SemaphoreType.DMA((10,)),
        ],
        compiler_params=pltpu.CompilerParams(
            collective_id=0, has_side_effects=True, vmem_limit_bytes=60 * 1024 * 1024
        ),
        name="selected",
    )(b[0], f[0], d[0], cf, e, idx, owner)
    return diag_p + quad_p, diag_c + quad_c


def solution(mesh):
    split_spec = P("leaf", "front", None)
    in_specs = (split_spec,) * 5 + (P(), P())
    out_specs = (P("leaf", None), P("leaf", None))
    return jax.shard_map(shards, mesh=mesh, in_specs=in_specs, out_specs=out_specs, check_vma=False)
```

```python
import jax
import jax.numpy as jnp
from jax import lax
from jax.experimental import pallas as pl
from jax.experimental.pallas import tpu as pltpu
from jax.sharding import PartitionSpec as P

F32 = jnp.float32
BF16 = jnp.bfloat16
MESH = pl.DeviceIdType.MESH


def dot(a, b):
    return jnp.dot(a, b, preferred_element_type=F32)


def dot3(ah, al, bh, bl):
    return dot(ah, bh) + (dot(ah, bl) + dot(al, bh))


def split(x):
    hi = x.astype(BF16)
    return hi, (x - hi.astype(F32)).astype(BF16)


def col_sum(x):
    return jnp.sum(x, axis=0, keepdims=True)


def select(flag, yes, no):
    return jnp.where(jnp.full(yes.shape, flag, jnp.int32) == 1, yes, no)


def kernel(
    b_in, f_in, d_in, cf_in, e_in, idx_in, owner_in,
    out_p, out_d, out_c, out_e,
    e_raw, c_raw, e_sel, c_sel,
    b_s, f_s, d_s, cf_s, e_s, k_s, v_s, u_s, w_half, w_s, w_x,
    idx_s, r_own, acc, owner,
    place, bh, bl, fh, fl, dh, dl, ch, cl, eh, el, kk, uh, ul, vh, vl, wh, wl, rh, rl, lh, ll,
    stage, fin, ostage, xfin, send, recv, loc,
):
    leaf = lax.axis_index("leaf")
    front = lax.axis_index("front")
    y = lax.div(front, 4)
    x = lax.rem(front, 4)
    core = lax.rem(leaf, 2)
    base = leaf - core
    partner = base + 1 - core
    group = lax.div(x, 2)
    pair = x + 1 - 2 * lax.rem(x, 2)
    col = 2 * lax.rem(x, 2) + core
    hub = core == group
    taken = [0, 0]

    def sends():
        taken[0] += 1
        return send.at[taken[0] - 1]

    def arrivals(n=1):
        taken[1] += n
        return recv.at[taken[1] - 1] if n == 1 else taken[1] - n

    def remote(src, dst, device, sent, arrived):
        return pltpu.make_async_remote_copy(
            src_ref=src, dst_ref=dst, send_sem=sent, recv_sem=arrived,
            device_id=device, device_id_type=MESH,
        )

    def wait(ref, sem):
        pltpu.make_async_copy(ref, ref, sem).wait()

    def at_y(p):
        return {"front": p * 4 + x}

    def on(chip, a_core=None):
        if a_core is None:
            return {"front": y * 4 + chip}
        return {"leaf": base + a_core, "front": y * 4 + chip}

    other_core = {"leaf": partner}

    rings, matrices = [], []

    class Ring:
        def __init__(self, part, span):
            right, left = lax.rem(y + 1, 4), lax.rem(y + 3, 4)
            self.span, self.sent = span, sends()
            self.near_sem, self.far_sem = arrivals(), arrivals()
            self.right = [
                remote(part(y, h), part(y, h), at_y(right), self.sent, at)
                for h, at in ((0, arrivals()), (1, self.near_sem))
            ]
            self.left = [
                remote(part(y, h), part(y, h), at_y(left), self.sent, at)
                for h, at in ((1, arrivals()), (0, self.near_sem))
            ]
            self.next_right = remote(part(left, 0), part(left, 0), at_y(right), self.sent, self.far_sem)
            self.next_left = remote(part(right, 1), part(right, 1), at_y(left), self.sent, self.far_sem)
            rings.append(self)

        def begin(self):
            for h in range(2):
                self.right[h].start()
                self.left[h].start()

        def relay(self):
            self.right[0].wait_recv()
            self.next_right.start()
            self.left[0].wait_recv()
            self.next_left.start()

        def near(self):
            wait(self.span(1), self.near_sem)

        def far(self):
            wait(self.span(1), self.far_sem)

        def finish(self):
            self.near()
            self.far()

        def end(self):
            wait(self.span(3), self.sent)

    class Rows:
        def __init__(self, part, whole, full, src, own, sem):
            self.whole, self.full = whole, full
            first = arrivals(3)
            goal = jnp.where(hub, pair, 3 - x)
            self.first_sent, self.next_sent, self.inside_sent = sends(), sends(), sends()
            self.pair_sem, self.next_sems, self.inside_sem = recv.at[first], [arrivals(), arrivals()], arrivals()
            self.first = [
                remote(src(h), part(x, h), on(goal), self.first_sent, recv.at[first + jnp.where(hub, 0, 1 + h)])
                for h in (0, 1)
            ]
            self.far_in = [(part(3 - x, h), recv.at[first + 1 + h]) for h in (0, 1)]
            self.next = [
                remote(part(3 - x, h), part(3 - x, h), on(pair), self.next_sent, self.next_sems[h])
                for h in (0, 1)
            ]
            self.inside = [
                remote(whole(p), whole(p), other_core, self.inside_sent, self.inside_sem)
                for p in (x, 3 - x, pair)
            ]
            self.last_in = [part(3 - pair, h) for h in (0, 1)]
            self.inside += [remote(ref, ref, other_core, self.inside_sent, self.inside_sem) for ref in self.last_in]
            self.local = pltpu.make_async_copy(own, whole(x), loc.at[sem])
            matrices.append(self)

        def begin(self):
            for h in range(2):
                self.first[h].start()

            @pl.when(hub)
            def _():
                self.local.start()

        def relay(self):
            @pl.when(hub)
            def _():
                self.local.wait()
                self.inside[0].start()
                for h in range(2):
                    wait(*self.far_in[h])
                    self.next[h].start()
                self.inside[1].start()

        def near(self):
            @pl.when(hub)
            def _():
                wait(self.whole(pair), self.pair_sem)
                self.inside[2].start()

        def pass_on(self):
            @pl.when(hub)
            def _():
                for h in range(2):
                    wait(self.last_in[h], self.next_sems[h])
                    self.inside[3 + h].start()

        def finish(self):
            @pl.when(jnp.logical_not(hub))
            def _():
                wait(self.full, self.inside_sem)

        def end(self):
            wait(self.whole(0), self.first_sent)

            @pl.when(hub)
            def _():
                wait(self.whole(0), self.next_sent)
                wait(self.full, self.inside_sent)

    def halves(ref, size, *lead):
        return lambda p, h: ref.at[(*lead, pl.ds(p * size + h * (size // 2), size // 2), slice(None))]

    def wholes(ref, size, *lead):
        return lambda p: ref.at[(*lead, pl.ds(p * size, size), slice(None))]

    def span(ref, size, *lead):
        return lambda n: ref.at[(*lead, pl.ds(0, size * n), slice(None))]

    def of(ref, size, lane=slice(None)):
        return lambda h: ref.at[pl.ds(h * (size // 2), size // 2), lane]

    lanes_768 = [pl.ds(0, 768), pl.ds(768, 768)]

    barrier = pltpu.get_barrier_semaphore()
    peers = [at_y(lax.rem(y + d, 4)) for d in (1, 2, 3)]
    row_peers = [on(lax.rem(x + d, 4), core) for d in (1, 3, 2)]
    row_peers += [on(lax.rem(x + d, 4), 1 - core) for d in (0, 1, 3, 2)]
    for peer in peers + row_peers:
        pl.semaphore_signal(barrier, inc=1, device_id=peer, device_id_type=MESH)

    def lanes(t):
        return pl.ds(pl.multiple_of(t * 128, 128), 128)

    def tiles(p):
        return lanes(p + lax.div(p + 1, 2)), lanes(1 + 3 * lax.div(p, 2))

    full_tile, half_tile = tiles(col)
    moves = [
        (idx_in.at[pl.ds(pl.multiple_of(lax.div(leaf, 4) * 8, 8), 8), :], idx_s),
        (owner_in, owner),
        (e_in, e_raw.at[0]),
        (cf_in, c_raw.at[0]),
    ]
    moves = [pltpu.make_async_copy(src, dst, loc.at[i]) for i, (src, dst) in enumerate(moves)]
    own_idx, own_owner, own_e, own_cf = moves
    for copy in (own_owner, own_e, own_cf, own_idx):
        copy.start()

    e_cross = remote(e_in, e_raw.at[1], other_core, sends(), arrivals())
    c_cross = remote(cf_in, c_raw.at[1], other_core, sends(), arrivals())

    def e_rows(p):
        return e_s.at[:, pl.ds(y * 128 + p * 32, 32), :]

    e_at = arrivals(4)
    e_across, is_own = [], []
    for j in range(4):
        is_own.append(jnp.logical_and(hub, col == j))
        e_across.append(remote(
            e_sel.at[:, :, lanes(j)], e_rows(x), on(2 * core + j // 2, j % 2), sends(), recv.at[e_at + x]
        ))
    e_kept = pltpu.make_async_copy(e_sel.at[:, :, lanes(col)], e_rows(x), loc.at[4])

    rows_d = Rows(halves(d_s, 48), wholes(d_s, 48), d_s, of(d_in, 48), d_in, 5)
    rows_c = Rows(
        lambda p, h: cf_s.at[h, pl.ds(p * 64, 64), :], lambda p: cf_s.at[:, pl.ds(p * 64, 64), :], cf_s,
        lambda h: c_sel.at[h], c_sel, 6,
    )
    rows_f = Rows(halves(f_s, 96), wholes(f_s, 96), f_s, of(f_in, 96), f_in, 7)
    rows_b = [
        Rows(halves(b_s, 96, c), wholes(b_s, 96, c), b_s.at[c], of(b_in, 96, lanes_768[c]), b_in.at[:, lanes_768[c]], 8 + c)
        for c in range(2)
    ]
    ring_e = Ring(lambda p, h: e_s.at[h, pl.ds(p * 128, 128), :], lambda n: e_s.at[:, pl.ds(0, 128 * n), :])
    ring_dp = Ring(halves(v_s, 288), span(v_s, 288))
    ring_k = [Ring(halves(k_s, 256, c), span(k_s, 256, c)) for c in range(2)]
    ring_w = Ring(halves(w_s, 576), span(w_s, 576))
    ring_v = Ring(
        lambda p, h: u_s.at[h, pl.ds(p * 192, 192), :], lambda n: u_s.at[:, pl.ds(0, 192 * n), :]
    )
    far_col = 2 * lax.rem(pair, 2) + core
    w_pair, w_in, w_on = [], [], []
    for rows in (pl.ds(0, 128), pl.ds(128, 128), pl.ds(256, 128), pl.ds(384, 192)):
        near, far = w_x.at[col, rows, :], w_x.at[far_col, rows, :]
        w_pair.append(remote(near, near, on(pair), sends(), arrivals()))
        w_in.append(remote(near, near, other_core, sends(), arrivals()))
        w_on.append(remote(far, far, other_core, sends(), arrivals()))

    pl.semaphore_wait(barrier, 10)

    e_cross.start()
    c_cross.start()
    rows_d.begin()

    def members(mine_leaf, other_leaf):
        pool = (2 * mine_leaf, 2 * mine_leaf + 1, 2 * other_leaf, 2 * other_leaf + 1)
        return pool, [(owner[p] == mine_leaf).astype(jnp.int32) for p in pool]

    def pick(c, flags, items):
        if c == 0:
            return select(flags[0], items[0], select(flags[1], items[1], items[2]))
        return select(flags[3], items[3], select(flags[2], items[2], items[1]))

    own_owner.wait()
    _, mine = members(leaf, partner)
    pool, held = members(base + group, base + 1 - group)
    own_e.wait()
    e_cross.wait_recv()
    for c in range(2):
        e_sel[c] = pick(c, mine, [e_raw[0, 0], e_raw[0, 1], e_raw[1, 0], e_raw[1, 1]])

    @pl.when(hub)
    def _():
        e_kept.start()

    for j in (2, 3, 0, 1):
        @pl.when(jnp.logical_not(is_own[j]))
        def _(j=j):
            e_across[j].start()

    rows_d.relay()
    own_cf.wait()
    c_cross.wait_recv()
    for c in range(2):
        for m in (0, 32):
            at = pl.ds(m, 32)
            c_sel[c, at, :] = pick(
                c, mine, [c_raw[0, 0, at, :], c_raw[0, 1, at, :], c_raw[1, 0, at, :], c_raw[1, 1, at, :]]
            )
    rows_c.begin()
    rows_d.near()

    own_idx.wait()
    idx_rows = [idx_s[pl.ds(lax.rem(p, 8), 1), :] for p in pool]

    def one_hot(c):
        positions = pick(c, held, idx_rows)
        for m in range(0, 2304, 128):
            at = lax.broadcasted_iota(jnp.int32, (128, 1024), 0) + m
            place[c, pl.ds(m, 128), :] = jnp.where(at == positions, 1.0, 0.0).astype(BF16)

    def split_rows(src, hi, lo, size, step):
        for m in range(0, size, step):
            h, l = split(src[pl.ds(m, step), :])
            hi[pl.ds(m, step), :] = h
            lo[pl.ds(m, step), :] = l

    def split_to(value, hi, lo, row, lane):
        h, l = split(value)
        hi[row, pl.ds(lane, 128)] = h
        lo[row, pl.ds(lane, 128)] = l

    def low_lanes(shape):
        return lax.broadcasted_iota(jnp.int32, shape, 1) < 64

    def swap(value):
        return pltpu.roll(value, 64, 1)

    def pack(top, bottom):
        return jnp.where(low_lanes(top.shape), top, swap(bottom))

    @pl.when(hub)
    def _():
        e_kept.wait()

    for p in range(4):
        @pl.when(jnp.logical_not(jnp.logical_and(hub, x == p)))
        def _(p=p):
            wait(e_rows(p), recv.at[e_at + p])

    ring_e.begin()
    rows_d.pass_on()
    rows_c.relay()
    rows_f.begin()
    ring_e.relay()

    rows_d.finish()
    whole = d_s[:, full_tile]
    half = d_s[:, half_tile]
    half = select(core, swap(half), half)
    d_sums = [col_sum(whole * whole), col_sum(half * half)]
    v_s[pl.ds(pl.multiple_of(y * 288, 96), 192), :] = whole
    v_s[pl.ds(pl.multiple_of(y * 288 + 192, 96), 96), :] = pack(half[:96], half[96:])
    ring_dp.begin()
    one_hot(0)
    rows_c.near()

    ring_e.finish()
    e_sums = []
    for c in range(2):
        for m in range(0, 512, 128):
            h, l = split(e_s[c, pl.ds(m, 128), :])
            eh[c, pl.ds(m, 128), :] = h
            el[c, pl.ds(m, 128), :] = l
        part = e_s[c, pl.ds(pl.multiple_of(y * 128, 128), 128), :]
        e_sums.append(col_sum(part * part))
    rows_f.relay()
    rows_c.pass_on()
    rows_c.finish()
    ring_dp.relay()
    for c in range(2):
        for m in range(0, 256, 64):
            h, l = split(cf_s[c, pl.ds(m, 64), :])
            ch[c, pl.ds(m, 64), :] = h
            cl[c, pl.ds(m, 64), :] = l
        for m in range(0, 256, 128):
            at = pl.ds(m, 128)
            k_s[c, pl.ds(pl.multiple_of(y * 256 + m, 128), 128), :] = dot3(ch[c, at, :], cl[c, at, :], eh[c], el[c])
        ring_k[c].begin()
    rows_b[0].begin()
    rows_f.near()
    one_hot(1)
    split_rows(d_s, dh, dl, 192, 48)

    ring_dp.finish()
    for p in range(4):
        for m in (0, 96):
            split_to(v_s[pl.ds(288 * p + m, 96), :], vh, vl, pl.ds(192 * p + m, 96), 0)
            value = v_s[pl.ds(288 * p + 192, 96), :]
            split_to(swap(value) if m else value, vh, vl, pl.ds(192 * p + m, 96), 128)
    ring_k[0].relay()
    rows_f.pass_on()
    rows_f.finish()
    split_rows(f_s, fh, fl, 384, 48)
    for m in (0, 192):
        at = pl.ds(m, 192)
        value = dot3(fh[at, :], fl[at, :], vh[...], vl[...])
        w_s[pl.ds(pl.multiple_of(y * 576 + m, 192), 192), :] = value[:, :128]
        w_half[at, :] = value[:, 128:]
    packed = pack(w_half[0:192, :], w_half[192:384, :])
    w_s[pl.ds(pl.multiple_of(y * 576 + 384, 192), 192), :] = packed
    ring_k[1].relay()
    ring_w.begin()
    rows_b[0].relay()
    rows_b[1].begin()

    v_sums = []
    for c in range(2):
        ring_k[c].finish()
        for m in range(0, 1024, 128):
            h, l = split(k_s[c, pl.ds(m, 128), :])
            kk[c, pl.ds(m, 128), pl.ds(0, 128)] = h
            kk[c, pl.ds(m, 128), pl.ds(128, 128)] = l
        cols = pl.ds(c * 128, 128)
        for m in range(0, 768, 256):
            at = pl.ds(m, 256)
            value = dot(place[c, at, :], kk[c]).astype(BF16)
            uh[at, cols] = value[:, :128]
            ul[at, cols] = value[:, 128:]
        if c == 0:
            ring_w.relay()
            rows_b[0].near()
            rows_b[1].relay()
        value = dot3(dh[...], dl[...], uh[:, cols], ul[:, cols])
        u_s[c, pl.ds(pl.multiple_of(y * 192, 192), 192), :] = value
        v_sums.append(col_sum(value * value))
    ring_v.begin()
    rows_b[0].pass_on()
    rows_b[1].near()
    for c in range(2):
        cols = pl.ds(c * 128, 128)
        for m in range(0, 1536, 256):
            at = pl.ds(m, 256)
            value = dot(place[c, pl.ds(768 + m, 256), :], kk[c]).astype(BF16)
            lh[at, cols] = value[:, :128]
            ll[at, cols] = value[:, 128:]
    rows_b[1].pass_on()

    def split_w(p):
        for m in (0, 192):
            row = pl.ds(pl.multiple_of(p * 384 + m, 192), 192)
            split_to(w_s[pl.ds(pl.multiple_of(p * 576 + m, 192), 192), :], rh, rl, row, 0)
            value = w_s[pl.ds(pl.multiple_of(p * 576 + 384, 192), 192), :]
            split_to(swap(value) if m else value, rh, rl, row, 128)

    def split_b(c):
        rows_b[c].finish()
        split_rows(b_s.at[c], bh.at[:, lanes_768[c]], bl.at[:, lanes_768[c]], 384, 48)

    split_b(0)
    split_w(y)
    ring_w.near()
    split_w(lax.rem(y + 1, 4))
    split_w(lax.rem(y + 3, 4))
    split_b(1)
    ring_w.far()
    split_w(lax.rem(y + 2, 4))
    p_sums = [jnp.zeros((1, 128), F32)] * 2
    for n in range(3):
        at = pl.ds(128 * n, 128)
        value = dot3(bh[at, :], bl[at, :], rh[...], rl[...])
        w_x[col, at, :] = value[:, :128]
        w_pair[n].start()
        w_in[n].start()
        to = pl.ds(pl.multiple_of(y * 576 + 128 * n, 64), 128)
        p_sums[0] = p_sums[0] + col_sum(value[:, :128] * w_s[to, :])
        p_sums[1] = p_sums[1] + col_sum(value[:, 128:] * w_half[at, :])
        w_half[at, :] = value[:, 128:]
    w_x[col, pl.ds(384, 192), :] = pack(w_half[0:192, :], w_half[192:384, :])
    w_pair[3].start()
    w_in[3].start()
    ring_v.relay()

    for m in range(0, 384, 128):
        at = pl.ds(m, 128)
        acc[at, :] = dot3(bh[at, :], bl[at, :], lh[...], ll[...])
    ring_v.finish()
    for c in range(2):
        for m in range(0, 768, 128):
            split_to(u_s[c, pl.ds(m, 128), :], vh, vl, pl.ds(m, 128), 128 * c)
    for m in range(0, 384, 128):
        at = pl.ds(m, 128)
        to = pl.ds(pl.multiple_of(y * 384 + m, 128), 128)
        value = lh[to, :].astype(F32) + ll[to, :].astype(F32)
        r_own[at, :] = value - dot3(fh[at, :], fl[at, :], vh[...], vl[...])
    for n in range(4):
        w_pair[n].wait_recv()
        w_on[n].start()
    for n in range(4):
        w_in[n].wait_recv()
        w_on[n].wait_recv()
    for p, t in enumerate((0, 2, 3, 5)):
        for m in (0, 192):
            split_to(w_x[p, pl.ds(m, 192), :], wh, wl, pl.ds(m, 192), 128 * t)
    for p, t in ((0, 1), (2, 4)):
        low, high = w_x[p, pl.ds(384, 192), :], w_x[p + 1, pl.ds(384, 192), :]
        split_to(jnp.where(low_lanes(low.shape), low, swap(high)), wh, wl, pl.ds(0, 192), 128 * t)
        split_to(jnp.where(low_lanes(low.shape), swap(low), high), wh, wl, pl.ds(192, 192), 128 * t)
    c_sums = v_sums
    for m in range(0, 384, 128):
        at = pl.ds(m, 128)
        value = acc[at, :] - dot3(wh[at, :], wl[at, :], uh[...], ul[...])
        value = col_sum(value * r_own[at, :])
        c_sums = [c_sums[c] + value[:, c * 128:(c + 1) * 128] for c in range(2)]

    for c in range(2):
        stage[c:c + 1, :] = p_sums[c]
        stage[2 + c:3 + c, :] = c_sums[c]
        stage[4 + c:5 + c, :] = d_sums[c]
        stage[6 + c:7 + c, :] = e_sums[c]
    fin[y] = stage[...]
    sent, arrived = sends(), arrivals()
    for d in (1, 3, 2):
        remote(stage, fin.at[y], at_y(lax.rem(y + d, 4)), sent, arrived).start()
    wait(fin.at[pl.ds(0, 3)], arrived)
    ostage[...] = ((fin[0] + fin[1]) + fin[2]) + fin[3]
    my_place = 4 * group + col
    xfin[my_place] = ostage[...]
    last_sent, arrived = sends(), arrivals()
    for peer in row_peers:
        remote(ostage, xfin.at[my_place], peer, last_sent, arrived).start()
    wait(xfin.at[pl.ds(0, 7)], arrived)
    before = 2 - mine[2] - mine[3]
    for j, t in enumerate((0, 2, 3, 5)):
        own, other = xfin[4 * core + j], xfin[4 - 4 * core + j]
        for ref, r in ((out_c, 2), (out_e, 6)):
            first = select(before, other[r + 1:r + 2], other[r:r + 1])
            ref[0:1, j * 128:(j + 1) * 128] = select(mine[0], own[r:r + 1], first)
            second = select(mine[0], own[r + 1:r + 2], own[r:r + 1])
            ref[1:2, j * 128:(j + 1) * 128] = select(mine[1], second, other[r + 1:r + 2])
        for ref, r in ((out_p, 0), (out_d, 4)):
            ref[:, t * 128:(t + 1) * 128] = own[r:r + 1]
            if j in (0, 2):
                after = xfin[4 * core + j + 1]
                ref[:, (t + 1) * 128:(t + 2) * 128] = pack(own[r + 1:r + 2], after[r + 1:r + 2])
    for each in rings + matrices:
        each.end()
    for copy in [e_cross, c_cross] + w_pair + w_in + w_on:
        copy.wait_send()
    for j in range(4):
        @pl.when(jnp.logical_not(is_own[j]))
        def _(j=j):
            e_across[j].wait_send()

    wait(fin.at[pl.ds(0, 3)], sent)
    wait(xfin.at[pl.ds(0, 7)], last_sent)
    assert taken == [SENDS, ARRIVALS], taken


SENDS, ARRIVALS = 41, 74


def shards(b, f, d, cf, e, idx, owner):
    vm = pltpu.VMEM
    any_spec = pl.BlockSpec(memory_space=pl.ANY)
    vmem_spec = pl.BlockSpec(memory_space=pltpu.VMEM)
    row, kid = jax.ShapeDtypeStruct((1, 768), F32), jax.ShapeDtypeStruct((2, 512), F32)
    quad_p, diag_p, quad_c, diag_c = pl.pallas_call(
        kernel,
        out_shape=(row, row, kid, kid),
        in_specs=[any_spec] * 7,
        out_specs=(vmem_spec,) * 4,
        scratch_shapes=[
            vm((2, 2, 32, 512), F32), vm((2, 2, 64, 512), F32), vm((2, 32, 512), F32), vm((2, 64, 512), F32),
            vm((2, 384, 768), F32), vm((384, 768), F32), vm((192, 768), F32),
            vm((2, 256, 512), F32), vm((2, 512, 128), F32),
            vm((2, 1024, 128), F32), vm((1152, 128), F32),
            vm((2, 768, 128), F32), vm((384, 128), F32), vm((2304, 128), F32), vm((4, 576, 128), F32),
            vm((8, 1024), jnp.int32), vm((384, 256), F32), vm((384, 256), F32),
            pltpu.SMEM((64,), jnp.int32),
            vm((2, 2304, 1024), BF16),
            vm((384, 1536), BF16), vm((384, 1536), BF16),
            vm((384, 768), BF16), vm((384, 768), BF16),
            vm((192, 768), BF16), vm((192, 768), BF16),
            vm((2, 256, 512), BF16), vm((2, 256, 512), BF16),
            vm((2, 512, 128), BF16), vm((2, 512, 128), BF16),
            vm((2, 1024, 256), BF16),
            vm((768, 256), BF16), vm((768, 256), BF16),
            vm((768, 256), BF16), vm((768, 256), BF16),
            vm((384, 768), BF16), vm((384, 768), BF16),
            vm((1536, 256), BF16), vm((1536, 256), BF16),
            vm((1536, 256), BF16), vm((1536, 256), BF16),
            vm((8, 128), F32), vm((4, 8, 128), F32), vm((8, 128), F32), vm((8, 8, 128), F32),
            pltpu.SemaphoreType.DMA((SENDS,)),
            pltpu.SemaphoreType.DMA((ARRIVALS,)),
            pltpu.SemaphoreType.DMA((10,)),
        ],
        compiler_params=pltpu.CompilerParams(
            collective_id=0, has_side_effects=True, vmem_limit_bytes=60 * 1024 * 1024
        ),
        name="selected",
    )(b[0], f[0], d[0], cf, e, idx, owner)
    return diag_p + quad_p, diag_c + quad_c


def solution(mesh):
    split_spec = P("leaf", "front", None)
    in_specs = (split_spec,) * 5 + (P(), P())
    out_specs = (P("leaf", None), P("leaf", None))
    return jax.shard_map(shards, mesh=mesh, in_specs=in_specs, out_specs=out_specs, check_vma=False)
```
